32 devices in a mesh: mesh: 4 (over z), modes: 8 (over y, x, core).
Axes of the slice: x: 2, y: 2, z: 4, core: 2. Of those that a mesh axis runs over, the one named last changes fastest.
Arguments:
- velocity: float32 [3, 128, 81, 512], P(None, 'modes', None, 'mesh'), may hold values from -2 to 2
- metrics: float32 [4, 512], P(None, 'mesh'), as said below
- connect: int32 [512, 4], P('mesh'), may hold values from -1 to 511, as said below
- send_list: int32 [8, 64], P('mesh'), may hold values from 0 to 127, as said below
- recv_slot: int32 [512, 2], P('mesh'), may hold values from -1 to 63, as said below
Outputs:
- new_velocity: float32 [3, 128, 81, 512], P(None, 'modes', None, 'mesh')
- advection: float32 [3, 128, 81, 512], P(None, 'modes', None, 'mesh')
The draws below stay inside these ranges and needn't reach their ends.
Inputs may be any that keep to these rules, and one draw needn't show every extreme that they name: Elements p * 128 to (p + 1) * 128 - 1 form partition p. connect[e, k] is the element across edge k of element e (0 bottom, 1 right, 2 top, 3 left), -1 where that edge is on the cylinder wall or the outer boundary; where recv_slot of that edge is -1 the neighbour lies in e's own partition, and neighbours across edges 1 and 3 always do. Row 2p (row 2p + 1) of send_list names, for each of the 64 edges shared with partition p - 1 (p + 1), the local index within partition p of the element whose bottom (top) edge it is; each row names 64 different elements. recv_slot[e, 0] is the column c such that the bottom neighbour of e is named by send_list[2p - 1, c] of partition p - 1, and -1 where that neighbour is in e's own partition or absent; recv_slot[e, 1] likewise for the top neighbour with send_list[2p + 2, c] of partition p + 1. `metrics`: rows 0 and 3 are positive stretches, rows 1 and 2 smaller shears.
All inputs are finite; a program needn't handle non-finite values.
Results may differ from the reference program's by a relative error of at most 0.0001.
Values sent between devices are 32-bit elements; how exact they have to be, the bound alone decides.
A program may use at most 192 MiB of HBM per device.

```python
import jax
import jax.numpy as jnp
import numpy as np
from jax import lax

COEF = 128
W = 64
RDEV = 2
ITERS = 2
E_DEV = 128
ELEMENTS = 512
N_MESH = 4


def partition_layout(key):
    part_keys = jax.random.split(key, N_MESH)
    slot_cells = jax.vmap(lambda part_key: jax.random.permutation(part_key, E_DEV))(part_keys).astype(jnp.int32)
    inverse = jnp.argsort(slot_cells, axis=1, stable=True).astype(jnp.int32)
    part_ids = jnp.arange(N_MESH, dtype=jnp.int32)[:, None]
    local_row = slot_cells // W
    column = slot_cells % W
    global_row = part_ids * RDEV + local_row
    cycle_count = RDEV * N_MESH

    def locate(cycle_rows, cycle_cols):
        inside = (cycle_rows >= 0) & (cycle_rows < cycle_count)
        clipped = jnp.clip(cycle_rows, 0, cycle_count - 1)
        owner_part = clipped // RDEV
        cell_index = clipped % RDEV * W + cycle_cols
        element_id = owner_part * E_DEV + inverse[owner_part, cell_index]
        return jnp.where(inside, element_id, -1).astype(jnp.int32)
    neighbours = jnp.stack([locate(global_row - 1, column), locate(global_row, (column + 1) % W), locate(global_row + 1, column), locate(global_row, (column + W - 1) % W)], axis=-1)
    connect = neighbours.reshape(ELEMENTS, 4)
    send_rows = jnp.stack([inverse[:, :W], inverse[:, (RDEV - 1) * W:]], axis=1).reshape(2 * N_MESH, W)
    lower_cols = jnp.where((local_row == 0) & (part_ids > 0), column, -1)
    upper_cols = jnp.where((local_row == RDEV - 1) & (part_ids < N_MESH - 1), column, -1)
    receive = jnp.stack([lower_cols, upper_cols], axis=-1).reshape(ELEMENTS, 2).astype(jnp.int32)
    return (connect, send_rows.astype(jnp.int32), receive)


def draw_connect(key, part):
    return partition_layout(jax.random.fold_in(key, 11))[0]


def draw_send_list(key, part):
    return partition_layout(jax.random.fold_in(key, 11))[1]


def draw_recv_slot(key, part):
    return partition_layout(jax.random.fold_in(key, 11))[2]


def draw_metrics(key, part):
    sub_keys = jax.random.split(key, 4)
    stretch_r = jax.random.uniform(sub_keys[0], (ELEMENTS,), jnp.float32, 0.7, 1.3)
    stretch_s = jax.random.uniform(sub_keys[3], (ELEMENTS,), jnp.float32, 0.7, 1.3)
    shear_r = jax.random.uniform(sub_keys[1], (ELEMENTS,), jnp.float32, -0.3, 0.3)
    shear_s = jax.random.uniform(sub_keys[2], (ELEMENTS,), jnp.float32, -0.3, 0.3)
    return jnp.stack([stretch_r, shear_r, shear_s, stretch_s]).astype(jnp.float32)


def block_levels(key, shape, pieces, low, largest):
    level, own = 1.0, jax.random.fold_in(key, 6)
    for dim, blocks in pieces:
        heights = jnp.exp(jax.random.uniform(jax.random.fold_in(own, dim), (blocks,), jnp.float32, low / len(pieces), largest / len(pieces)))
        level = level * jnp.repeat(heights, shape[dim] // blocks).reshape([-1 if axis == dim else 1 for axis in range(len(shape))])
    return level


def normal_values(key, extent, width, limit, cuts=(), kind=jnp.bfloat16):
    drawn = width * jax.random.normal(key, extent, jnp.float32)
    if cuts:
        drawn = drawn * block_levels(key, extent, cuts, -0.22, 0.18)
    return jnp.clip(drawn, -limit, limit).astype(kind)


def setup_inputs(seed: int = 0) -> dict:
    arg_keys = jax.random.split(jax.random.key(seed), 6)
    velocity = normal_values(arg_keys[0], (3, COEF, 81, ELEMENTS), 0.15, 2.0, ((1, 8), (3, 4)), jnp.float32)
    metrics = draw_metrics(jax.random.fold_in(arg_keys[5], 71), 0)
    connect = draw_connect(jax.random.fold_in(arg_keys[5], 71), 0)
    send_list = draw_send_list(jax.random.fold_in(arg_keys[5], 71), 0)
    recv_slot = draw_recv_slot(jax.random.fold_in(arg_keys[5], 71), 0)
    return {"velocity": velocity, "metrics": metrics, "connect": connect, "send_list": send_list, "recv_slot": recv_slot}


highest = lax.Precision.HIGHEST
helm_shift = 4.0
penalty_weight = 200.0
spectral_bound = 400.0
relaxation = 0.8
time_step = 0.02
wave_scale = 0.125
gll_interior = [-0.8997579954114602, -0.6771862795107377, -0.3631174638261782, 0.0, 0.3631174638261782, 0.6771862795107377, 0.8997579954114602]


def legendre_value(point, degree):
    previous = 1.0
    current = point
    for order_index in range(1, degree):
        following = ((2 * order_index + 1) * point * current - order_index * previous) / (order_index + 1)
        previous = current
        current = following
    return current


def spectral_tables(coef_count):
    poly_order = 8
    node_count = poly_order + 1
    points = np.array([-1.0] + gll_interior + [1.0])
    values = np.array([legendre_value(points[node], poly_order) for node in range(node_count)])
    derivative = np.zeros((node_count, node_count))
    for row_index in range(node_count):
        for col_index in range(node_count):
            if row_index != col_index:
                derivative[row_index, col_index] = values[row_index] / (values[col_index] * (points[row_index] - points[col_index]))
    derivative[0, 0] = -poly_order * (poly_order + 1) / 4.0
    derivative[poly_order, poly_order] = poly_order * (poly_order + 1) / 4.0
    identity = np.eye(node_count)
    along_r = np.kron(identity, derivative)
    along_s = np.kron(derivative, identity)
    second = np.stack([along_r @ along_r, along_r @ along_s, along_s @ along_s])
    line_nodes = np.arange(node_count)
    edge_nodes = np.stack([line_nodes, line_nodes * node_count + poly_order, poly_order * node_count + line_nodes, line_nodes * node_count])
    scatter_edge = np.zeros((node_count * node_count, 4 * node_count))
    for edge_index in range(4):
        scatter_edge[edge_nodes[edge_index], edge_index * node_count + line_nodes] = 1.0
    planes = np.arange(coef_count) * 2.0 * np.pi / coef_count
    half_count = coef_count // 2
    wavenumber = np.zeros(coef_count)
    basis = np.zeros((coef_count, coef_count))
    z_derivative = np.zeros((coef_count, coef_count))
    basis[:, 0] = 1.0
    basis[:, 1] = np.cos(half_count * planes)
    wavenumber[1] = half_count
    for mode_number in range(1, half_count):
        basis[:, 2 * mode_number] = np.cos(mode_number * planes)
        basis[:, 2 * mode_number + 1] = np.sin(mode_number * planes)
        wavenumber[2 * mode_number] = mode_number
        wavenumber[2 * mode_number + 1] = mode_number
        z_derivative[2 * mode_number, 2 * mode_number + 1] = wave_scale * mode_number
        z_derivative[2 * mode_number + 1, 2 * mode_number] = -wave_scale * mode_number
    norms = np.full(coef_count, coef_count / 2.0)
    norms[0] = coef_count
    norms[1] = coef_count
    inverse = basis.T / norms[:, None]
    shifts = helm_shift + (wave_scale * wavenumber) ** 2
    plane_derivative = basis @ z_derivative @ inverse
    float_tables = [jnp.asarray(table, dtype=jnp.float32) for table in (along_r, along_s, second, scatter_edge, basis, inverse, z_derivative, shifts, plane_derivative)]
    return float_tables, edge_nodes


def element_factors(metrics):
    return jnp.stack([metrics[0] * metrics[0] + metrics[1] * metrics[1], 2.0 * (metrics[0] * metrics[2] + metrics[1] * metrics[3]), metrics[2] * metrics[2] + metrics[3] * metrics[3]])


def laplacian(field, factors, second):
    total = factors[0] * jnp.einsum("qr,fcre->fcqe", second[0], field, precision=highest)
    total = total + factors[1] * jnp.einsum("qr,fcre->fcqe", second[1], field, precision=highest)
    total = total + factors[2] * jnp.einsum("qr,fcre->fcqe", second[2], field, precision=highest)
    return total


def reference(velocity, metrics, connect, send_list, recv_slot):
    float_tables, edge_nodes = spectral_tables(COEF)
    along_r, along_s, second, scatter_edge, basis, inverse, z_derivative, shifts, plane_derivative = float_tables
    element_total = velocity.shape[3]
    blocks = velocity.reshape(3, COEF, 81, N_MESH, E_DEV).transpose(3, 0, 1, 2, 4)
    metric_blocks = metrics.reshape(4, N_MESH, E_DEV).transpose(1, 0, 2)

    def advect(paired):
        vel_block, met_block = paired
        grad_r = jnp.einsum("qr,fcre->fcqe", along_r, vel_block, precision=highest)
        grad_s = jnp.einsum("qr,fcre->fcqe", along_s, vel_block, precision=highest)
        grad_x = met_block[0] * grad_r + met_block[2] * grad_s
        grad_y = met_block[1] * grad_r + met_block[3] * grad_s
        grad_z = jnp.einsum("cd,fdqe->fcqe", z_derivative, vel_block, precision=highest)
        stacked = jnp.concatenate([vel_block, grad_x, grad_y, grad_z], axis=0)
        physical = jnp.einsum("pc,fcqe->fpqe", basis, stacked, precision=highest)
        term = physical[0] * physical[3:6] + physical[1] * physical[6:9] + physical[2] * physical[9:12]
        return jnp.einsum("cp,fpqe->fcqe", inverse, term, precision=highest)

    advected = lax.map(advect, (blocks, metric_blocks))
    advection = advected.transpose(1, 2, 3, 0, 4).reshape(3, COEF, 81, element_total)

    factors = element_factors(metrics)
    precond = shifts[:, None] + spectral_bound * (factors[0] + factors[2])[None, :] + penalty_weight
    part_of = jnp.arange(element_total, dtype=jnp.int32) // E_DEV
    has_local = (connect >= 0).astype(jnp.float32)
    picks = jnp.clip(connect, 0, element_total - 1)
    width_cols = send_list.shape[1]
    lower_cols = recv_slot[:, 0]
    upper_cols = recv_slot[:, 1]
    lower_source = part_of - 1
    lower_valid = (lower_source >= 0).astype(jnp.float32)
    lower_clip = jnp.clip(lower_source, 0, N_MESH - 1)
    lower_sender = lower_clip * E_DEV + send_list[2 * lower_clip + 1, jnp.clip(lower_cols, 0, width_cols - 1)]
    upper_source = part_of + 1
    upper_valid = (upper_source < N_MESH).astype(jnp.float32)
    upper_clip = jnp.clip(upper_source, 0, N_MESH - 1)
    upper_sender = upper_clip * E_DEV + send_list[2 * upper_clip, jnp.clip(upper_cols, 0, width_cols - 1)]
    opposite = [2, 3, 0, 1]

    def operator(field):
        traces = field[:, :, edge_nodes, :]
        nearby = []
        for edge_index in range(4):
            nearby.append(jnp.take(traces[:, :, opposite[edge_index]], picks[:, edge_index], axis=-1) * has_local[:, edge_index])
        nearby[0] = jnp.where(lower_cols >= 0, jnp.take(traces[:, :, 2], lower_sender, axis=-1) * lower_valid, nearby[0])
        nearby[2] = jnp.where(upper_cols >= 0, jnp.take(traces[:, :, 0], upper_sender, axis=-1) * upper_valid, nearby[2])
        neighbours = jnp.stack(nearby, axis=2)
        differences = (traces - neighbours).reshape(field.shape[0], field.shape[1], 36, field.shape[3])
        penalty = jnp.einsum("qt,fcte->fcqe", scatter_edge, differences, precision=highest)
        return shifts[:, None, None] * field - laplacian(field, factors, second) + penalty_weight * penalty

    right_side = helm_shift * (velocity - time_step * advection)
    state = velocity
    for sweep in range(ITERS):
        applied = operator(state)
        state = state + relaxation * (right_side - applied) / precond[:, None, :]
    return state, advection
```

```python
import functools

import jax
import jax.numpy as jnp
import ml_dtypes
import numpy as np
from jax import lax
from jax.experimental import pallas as pl
from jax.experimental.pallas import tpu as pltpu
from jax.sharding import PartitionSpec as P

COEF = 128
LANES = 128


highest = lax.Precision.HIGHEST
helm_shift = 4.0
penalty_weight = 200.0
spectral_bound = 400.0
relaxation = 0.8
time_step = 0.02
wave_scale = 0.125
gll_interior = [
    -0.8997579954114602,
    -0.6771862795107377,
    -0.3631174638261782,
    0.0,
    0.3631174638261782,
    0.6771862795107377,
    0.8997579954114602,
]


def shifted(block, axis, distance):
    devices = range(lax.axis_size(axis))
    route = [(i - distance, i) for i in devices if i - distance in devices]
    return lax.ppermute(block, axis, route)


def legendre_value(point, degree):
    previous = 1.0
    current = point
    for order_index in range(1, degree):
        following = ((2 * order_index + 1) * point * current - order_index * previous) / (
            order_index + 1
        )
        previous = current
        current = following
    return current


def spectral_tables(coef_count):
    poly_order = 8
    node_count = poly_order + 1
    points = np.array([-1.0] + gll_interior + [1.0])
    values = np.array([legendre_value(points[node], poly_order) for node in range(node_count)])
    derivative = np.zeros((node_count, node_count))
    for row_index in range(node_count):
        for col_index in range(node_count):
            if row_index != col_index:
                derivative[row_index, col_index] = values[row_index] / (
                    values[col_index] * (points[row_index] - points[col_index])
                )
    derivative[0, 0] = -poly_order * (poly_order + 1) / 4.0
    derivative[poly_order, poly_order] = poly_order * (poly_order + 1) / 4.0
    identity = np.eye(node_count)
    along_r = np.kron(identity, derivative)
    along_s = np.kron(derivative, identity)
    second = np.stack([along_r @ along_r, along_r @ along_s, along_s @ along_s])
    line_nodes = np.arange(node_count)
    edge_nodes = np.stack(
        [
            line_nodes,
            line_nodes * node_count + poly_order,
            poly_order * node_count + line_nodes,
            line_nodes * node_count,
        ]
    )
    counts = np.zeros(node_count * node_count)
    for edge_index in range(4):
        counts[edge_nodes[edge_index]] += 1.0
    planes = np.arange(coef_count) * 2.0 * np.pi / coef_count
    half_count = coef_count // 2
    wavenumber = np.zeros(coef_count)
    basis = np.zeros((coef_count, coef_count))
    z_derivative = np.zeros((coef_count, coef_count))
    basis[:, 0] = 1.0
    basis[:, 1] = np.cos(half_count * planes)
    wavenumber[1] = half_count
    for mode_number in range(1, half_count):
        basis[:, 2 * mode_number] = np.cos(mode_number * planes)
        basis[:, 2 * mode_number + 1] = np.sin(mode_number * planes)
        wavenumber[2 * mode_number] = mode_number
        wavenumber[2 * mode_number + 1] = mode_number
        z_derivative[2 * mode_number, 2 * mode_number + 1] = wave_scale * mode_number
        z_derivative[2 * mode_number + 1, 2 * mode_number] = -wave_scale * mode_number
    norms = np.full(coef_count, coef_count / 2.0)
    norms[0] = coef_count
    norms[1] = coef_count
    inverse = basis.T / norms[:, None]
    shifts = helm_shift + (wave_scale * wavenumber) ** 2
    return along_r, along_s, second, counts, basis, inverse, z_derivative, shifts


def split_table(table):
    exact = np.asarray(table, np.float64).astype(np.float32)
    high = exact.astype(ml_dtypes.bfloat16)
    low = (exact - high.astype(np.float32)).astype(ml_dtypes.bfloat16)
    return high, low


def pad_table(table, rows, cols):
    out = np.zeros((rows, cols))
    out[: table.shape[0], : table.shape[1]] = table
    return out


def split_value(value):
    high = value.astype(jnp.bfloat16)
    low = (value - high.astype(jnp.float32)).astype(jnp.bfloat16)
    return high, low


def mul(a, b):
    return jnp.dot(a, b, preferred_element_type=jnp.float32)


def row_ids():
    return lax.broadcasted_iota(jnp.int32, (8, LANES), 0)


def lane_ids():
    return lax.broadcasted_iota(jnp.int32, (8, LANES), 1)


def lane_take(value, index):
    return jnp.take_along_axis(value, index, axis=1, mode="promise_in_bounds")


def table_row(ref, row):
    return jnp.broadcast_to(ref[row : row + 1, :], (8, LANES))


def load_tile(ref, field, tile):
    if tile < 10:
        return ref[0, field, 8 * tile : 8 * tile + 8, :]
    last = jnp.broadcast_to(ref[0, field, 80:81, :], (8, LANES))
    return jnp.where(row_ids() == 0, last, 0.0)


def store_tile(ref, field, tile, value):
    if tile < 10:
        ref[0, field, 8 * tile : 8 * tile + 8, :] = value
    else:
        ref[0, field, 80:81, :] = value[0:1, :]


def swap_groups(planes):
    group = lane_ids() // 16
    planes = list(planes)
    for bit in (1, 2, 4):
        upper = (group & bit) != 0
        for i in range(8):
            if i & bit:
                continue
            j = i | bit
            first, second = planes[i], planes[j]
            planes[i] = jnp.where(upper, pltpu.roll(second, 16 * bit, 1), first)
            planes[j] = jnp.where(upper, second, pltpu.roll(first, LANES - 16 * bit, 1))
    return planes


def emit_halo(field_ref, table_ref, down_ref, up_ref, fields):
    pairs = fields // 2
    left = lane_ids() < 64
    for ref, table, base in ((down_ref, 6, 0), (up_ref, 7, 72)):
        index = table_row(table_ref, table)
        for pair in range(pairs):
            a, b = 2 * pair, 2 * pair + 1
            main = jnp.where(
                left,
                lane_take(field_ref[0, a, base : base + 8, :], index),
                lane_take(field_ref[0, b, base : base + 8, :], index),
            )
            ref[0, 8 * pair : 8 * pair + 8, :] = main
            rest_a = jnp.broadcast_to(field_ref[0, a, base + 8 : base + 9, :], (8, LANES))
            rest_b = jnp.broadcast_to(field_ref[0, b, base + 8 : base + 9, :], (8, LANES))
            rest = jnp.where(left, lane_take(rest_a, index), lane_take(rest_b, index))
            ref[0, 8 * pairs + pair : 8 * pairs + pair + 1, :] = rest[0:1, :]


def factor_rows(metrics_ref):
    rx, ry, sx, sy = (table_row(metrics_ref, k) for k in range(4))
    return rx * rx + ry * ry, 2.0 * (rx * sx + ry * sy), sx * sx + sy * sy


def pack_kernel(fields, packed, table_ref, x_ref, *outs):
    if packed:
        out_ref, down_ref, up_ref = outs
        for block in range(fields // 8):
            for tile in range(11):
                planes = swap_groups([load_tile(x_ref, 8 * block + g, tile) for g in range(8)])
                for g in range(8):
                    start = 88 * block + 8 * tile
                    out_ref[g, start : start + 8, :] = planes[g]
    else:
        down_ref, up_ref = outs
    emit_halo(x_ref, table_ref, down_ref, up_ref, fields)


def apply_operator(
    fields, shift_ref, metrics_ref, table_ref, ah_ref, al_ref, diag_ref, x_ref, low_ref, top_ref, finish
):
    pairs = fields // 2
    start = lax.axis_index("modes") * fields
    fa, fb, fc = factor_rows(metrics_ref)
    base = spectral_bound * (fa + fc) + penalty_weight
    raw = [table_row(table_ref, k) for k in range(6)]
    index = [jnp.maximum(r, 0) for r in raw]
    valid = [r >= 0 for r in raw]
    rows = row_ids()

    def pair_step(pair, carry):
        tiles = [[load_tile(x_ref, 2 * pair + h, t) for t in range(11)] for h in range(2)]
        zero = jnp.zeros((8, LANES), jnp.float32)
        both = jnp.concatenate(
            [jnp.concatenate(tiles[h] + [zero], axis=0) for h in range(2)], axis=1
        )
        high, low = split_value(both)
        ah, al = ah_ref[...], al_ref[...]
        second = mul(ah, high) + (mul(ah, low) + mul(al, high))
        low_main = low_ref[0, pl.ds(pl.multiple_of(8 * pair, 8), 8), :]
        top_main = top_ref[0, pl.ds(pl.multiple_of(8 * pair, 8), 8), :]
        low_rest = jnp.broadcast_to(low_ref[0, pl.ds(8 * pairs + pair, 1), :], (8, LANES))
        top_rest = jnp.broadcast_to(top_ref[0, pl.ds(8 * pairs + pair, 1), :], (8, LANES))
        for h in range(2):
            x = tiles[h]
            field = 2 * pair + h
            shift = shift_ref[start + field]
            scale = relaxation / (base + shift)
            low_index = index[4] + 64 * h
            top_index = index[5] + 64 * h

            def bottom(source, halo):
                own = jnp.where(valid[0], lane_take(source, index[0]), 0.0)
                return jnp.where(valid[4], lane_take(halo, low_index), own)

            def top(source, halo):
                own = jnp.where(valid[2], lane_take(source, index[2]), 0.0)
                return jnp.where(valid[5], lane_take(halo, top_index), own)

            for t in range(11):
                near = zero
                if t > 0 and t != 9:
                    right = jnp.where(valid[1], lane_take(x[t - 1], index[1]), 0.0)
                    near = near + jnp.where((rows + 8 * t) % 9 == 8, right, 0.0)
                if t < 8 or t == 9:
                    left = jnp.where(valid[3], lane_take(x[t + 1], index[3]), 0.0)
                    near = near + jnp.where((rows + 8 * t) % 9 == 0, left, 0.0)
                if t == 0:
                    near = near + bottom(x[9], low_main)
                if t == 1:
                    near = near + jnp.where(rows == 0, bottom(x[10], low_rest), 0.0)
                if t == 9:
                    near = near + top(x[0], top_main)
                if t == 10:
                    near = near + jnp.where(rows == 0, top(x[1], top_rest), 0.0)
                lanes = slice(LANES * h, LANES * h + LANES)
                lap = (
                    fa * second[8 * t : 8 * t + 8, lanes]
                    + fb * second[88 + 8 * t : 96 + 8 * t, lanes]
                    + fc * second[176 + 8 * t : 184 + 8 * t, lanes]
                )
                count = diag_ref[8 * t : 8 * t + 8, :]
                applied = shift * x[t] - lap + penalty_weight * (count * x[t] - near)
                finish(field, t, x[t], applied, scale)
        return carry

    lax.fori_loop(0, pairs, pair_step, 0)


def first_kernel(
    fields, shift_ref, metrics_ref, table_ref, ah_ref, al_ref, diag_ref, x_ref, low_ref, top_ref, out_ref
):
    def finish(field, tile, x, applied, scale):
        store_tile(out_ref, field, tile, x + scale * (helm_shift * x - applied))

    apply_operator(
        fields, shift_ref, metrics_ref, table_ref, ah_ref, al_ref, diag_ref, x_ref, low_ref, top_ref, finish
    )


def last_kernel(
    fields,
    shift_ref,
    metrics_ref,
    table_ref,
    ah_ref,
    al_ref,
    diag_ref,
    x_ref,
    low_ref,
    top_ref,
    vel_ref,
    adv_ref,
    out_ref,
):
    def finish(field, tile, x, applied, scale):
        right = helm_shift * (
            load_tile(vel_ref, field, tile) - time_step * load_tile(adv_ref, field, tile)
        )
        store_tile(out_ref, field, tile, x + scale * (right - applied))

    apply_operator(
        fields, shift_ref, metrics_ref, table_ref, ah_ref, al_ref, diag_ref, x_ref, low_ref, top_ref, finish
    )


def state_kernel(fields, packed, shift_ref, metrics_ref, table_ref, adv_in_ref, part_ref, *outs):
    start = lax.axis_index("modes") * fields
    fa, _, fc = factor_rows(metrics_ref)
    base = spectral_bound * (fa + fc) + penalty_weight
    amount = relaxation * helm_shift * time_step
    if packed:
        adv_ref, state_ref, down_ref, up_ref = outs
        for block in range(fields // 8):
            weight = [amount / (base + shift_ref[start + 8 * block + g]) for g in range(8)]
            for tile in range(11):
                first = 88 * block + 8 * tile
                planes = swap_groups([adv_in_ref[g, first : first + 8, :] for g in range(8)])
                for g in range(8):
                    field = 8 * block + g
                    store_tile(adv_ref, field, tile, planes[g])
                    part = load_tile(part_ref, field, tile)
                    store_tile(state_ref, field, tile, part - weight[g] * planes[g])
    else:
        state_ref, down_ref, up_ref = outs
        for field in range(fields):
            weight = amount / (base + shift_ref[start + field])
            for tile in range(11):
                part = load_tile(part_ref, field, tile)
                store_tile(
                    state_ref, field, tile, part - weight * load_tile(adv_in_ref, field, tile)
                )
    emit_halo(state_ref, table_ref, down_ref, up_ref, fields)


def plane_kernel(
    metrics_ref, bh_ref, bl_ref, dh_ref, dl_ref, ih_ref, il_ref, in_ref, out_ref, y0, y1, y2
):
    stages = (y0, y1, y2)
    offset = lax.axis_index("modes") * 16

    def spread(source, carry):
        for f in range(3):
            for block in range(2):
                first = 88 * (2 * f + block)
                part = in_ref[source, first : first + 88, :]
                full = jnp.concatenate([part, jnp.zeros((40, LANES), jnp.float32)], axis=0)
                where = pl.multiple_of(source * 256 + block * 128, 128)
                stages[f][pl.ds(where, 128), :] = full.T
        return carry

    lax.fori_loop(0, 8, spread, 0)

    def element(e, carry):
        value = jnp.concatenate(
            [stages[f][pl.ds(e, 128, stride=16), :] for f in range(3)], axis=1
        )
        high, low = split_value(value)
        planes = mul(bh_ref[...], jnp.concatenate([high, low], axis=0)) + mul(bl_ref[...], high)
        u, v, w = (planes[:128, 128 * f : 128 * f + 128] for f in range(3))
        high, low = split_value(jnp.concatenate([u, v, w], axis=0))
        grads = mul(jnp.concatenate([high, low], axis=1), dh_ref[...]) + mul(high, dl_ref[...])
        rx, ry, sx, sy = (metrics_ref[k, offset + e] for k in range(4))
        along_r = rx * u + ry * v
        along_s = sx * u + sy * v
        terms = []
        for f in range(3):
            rows = slice(128 * f, 128 * f + 128)
            terms.append(
                along_r * grads[rows, :128]
                + along_s * grads[rows, 128:]
                + w * planes[128:, 128 * f : 128 * f + 128]
            )
        high, low = split_value(jnp.concatenate(terms, axis=1))
        back = mul(ih_ref[...], jnp.concatenate([high, low], axis=0)) + mul(il_ref[...], high)
        for f in range(3):
            stages[f][pl.ds(e, 128, stride=16), :] = back[:, 128 * f : 128 * f + 128]
        return carry

    lax.fori_loop(0, 16, element, 0)

    def gather(target, carry):
        for f in range(3):
            for block in range(2):
                first = 88 * (2 * f + block)
                where = pl.multiple_of(target * 256 + block * 128, 128)
                full = stages[f][pl.ds(where, 128), :]
                out_ref[target, first : first + 88, :] = full.T[:88, :]
        return carry

    lax.fori_loop(0, 8, gather, 0)


def plain_advection(velocity, metrics, tables, mode_count):
    along_r, along_s, basis, inverse, plane_z = tables
    share = velocity.shape[3] // mode_count
    mode_index = lax.axis_index("modes")
    local = lax.dynamic_slice_in_dim(metrics, mode_index * share, share, axis=1)
    field = lax.all_to_all(velocity, "modes", split_axis=3, concat_axis=1, tiled=True)
    physical = jnp.einsum("pc,fcqe->fpqe", basis, field, precision=highest)
    grad_z = jnp.einsum("pc,fcqe->fpqe", plane_z, field, precision=highest)
    grad_r = jnp.einsum("qr,fpre->fpqe", along_r, physical, precision=highest)
    grad_s = jnp.einsum("qr,fpre->fpqe", along_s, physical, precision=highest)
    grad_x = local[0] * grad_r + local[2] * grad_s
    grad_y = local[1] * grad_r + local[3] * grad_s
    term = physical[0] * grad_x + physical[1] * grad_y + physical[2] * grad_z
    spectral = jnp.einsum("cp,fpqe->fcqe", inverse, term, precision=highest)
    return lax.all_to_all(spectral, "modes", split_axis=1, concat_axis=3, tiled=True)


def body(velocity, metrics, connect, send_list, recv_slot):
    along_r, along_s, second, counts, basis, inverse, z_derivative, shifts = spectral_tables(COEF)
    mode_count = lax.axis_size("modes")
    mesh_index = lax.axis_index("mesh")
    fields = velocity.shape[1]
    elements = velocity.shape[3]
    packed = mode_count == 8
    own = jnp.where(
        connect < 0, -1, jnp.clip(connect - mesh_index * elements, 0, elements - 1)
    )
    table = jnp.concatenate(
        [own.T, recv_slot.T, jnp.concatenate([send_list, send_list], axis=1)], axis=0
    )
    shifts = jnp.asarray(shifts, jnp.float32)
    halo_rows = 8 * (fields // 2) + (fields // 2 + 7) // 8 * 8
    ah, al = split_table(
        np.concatenate([pad_table(second[k], 88, 96) for k in range(3)], axis=0)
    )
    diag = np.zeros((88, LANES), np.float32)
    diag[:81] = counts[:, None]

    field_shape = jax.ShapeDtypeStruct(velocity.shape, jnp.float32)
    halo_shape = jax.ShapeDtypeStruct((3, halo_rows, LANES), jnp.float32)
    pack_shape = jax.ShapeDtypeStruct((8, 6 * 88, LANES), jnp.float32)
    field_spec = pl.BlockSpec((1, fields, 81, LANES), lambda f: (f, 0, 0, 0))
    halo_spec = pl.BlockSpec((1, halo_rows, LANES), lambda f: (f, 0, 0))
    pack_spec = pl.BlockSpec((8, 176, LANES), lambda f: (0, f, 0))
    smem = pl.BlockSpec(memory_space=pltpu.SMEM)

    def whole(shape):
        return pl.BlockSpec(shape, lambda f: (0,) * len(shape))

    params = pltpu.CompilerParams(vmem_limit_bytes=48 << 20)
    metric_spec, table_spec = whole((4, LANES)), whole((8, LANES))
    operator_specs = [
        smem,
        metric_spec,
        table_spec,
        whole((264, 96)),
        whole((264, 96)),
        whole((88, LANES)),
        field_spec,
        halo_spec,
        halo_spec,
    ]
    operator_tables = (shifts, metrics, table, jnp.asarray(ah), jnp.asarray(al), jnp.asarray(diag))

    sent = pl.pallas_call(
        functools.partial(pack_kernel, fields, packed),
        grid=(3,),
        in_specs=[table_spec, field_spec],
        out_specs=([pack_spec] if packed else []) + [halo_spec, halo_spec],
        out_shape=([pack_shape] if packed else []) + [halo_shape, halo_shape],
        compiler_params=params,
    )(table, velocity)
    down, up = sent[-2:]
    if packed:
        moved = lax.all_to_all(sent[0], "modes", split_axis=0, concat_axis=0, tiled=True)
    low = shifted(up, "mesh", 1)
    top = shifted(down, "mesh", -1)
    part = pl.pallas_call(
        functools.partial(first_kernel, fields),
        grid=(3,),
        in_specs=operator_specs,
        out_specs=field_spec,
        out_shape=field_shape,
        compiler_params=params,
        cost_estimate=pl.CostEstimate(
            flops=2 * 10**9, bytes_accessed=4 * 10**6, transcendentals=0
        ),
    )(*operator_tables, velocity, low, top)

    plane_z = basis @ z_derivative
    if packed:
        bh, bl = split_table(np.concatenate([basis, plane_z], axis=0))
        dh, dl = split_table(
            np.concatenate(
                [pad_table(along_r.T, 128, 128), pad_table(along_s.T, 128, 128)], axis=1
            )
        )
        ih, il = split_table(inverse)
        vmem = pl.BlockSpec(memory_space=pltpu.VMEM)
        terms = pl.pallas_call(
            plane_kernel,
            in_specs=[smem] + [vmem] * 7,
            out_specs=vmem,
            out_shape=pack_shape,
            scratch_shapes=[pltpu.VMEM((2048, LANES), jnp.float32)] * 3,
            compiler_params=params,
        )(
            metrics,
            jnp.asarray(np.concatenate([bh, bh], axis=1)),
            jnp.asarray(bl),
            jnp.asarray(np.concatenate([dh, dh], axis=0)),
            jnp.asarray(dl),
            jnp.asarray(np.concatenate([ih, ih], axis=1)),
            jnp.asarray(il),
            moved,
        )
        adv_in = lax.all_to_all(terms, "modes", split_axis=0, concat_axis=0, tiled=True)
        adv_spec = pack_spec
    else:
        tables = [
            jnp.asarray(t, jnp.float32) for t in (along_r, along_s, basis, inverse, plane_z)
        ]
        adv_in = plain_advection(velocity, metrics, tables, mode_count)
        adv_spec = field_spec

    found = pl.pallas_call(
        functools.partial(state_kernel, fields, packed),
        grid=(3,),
        in_specs=[smem, metric_spec, table_spec, adv_spec, field_spec],
        out_specs=([field_spec] if packed else []) + [field_spec, halo_spec, halo_spec],
        out_shape=([field_shape] if packed else []) + [field_shape, halo_shape, halo_shape],
        compiler_params=params,
    )(shifts, metrics, table, adv_in, part)
    advection = found[0] if packed else adv_in
    state, down, up = found[-3:]
    low = shifted(up, "mesh", 1)
    top = shifted(down, "mesh", -1)
    new_velocity = pl.pallas_call(
        functools.partial(last_kernel, fields),
        grid=(3,),
        in_specs=operator_specs + [field_spec, field_spec],
        out_specs=field_spec,
        out_shape=field_shape,
        compiler_params=params,
    )(*operator_tables, state, low, top, velocity, advection)
    return (new_velocity, advection)


def solution(mesh):
    return jax.shard_map(
        body,
        mesh=mesh,
        in_specs=(
            P(None, "modes", None, "mesh"),
            P(None, "mesh"),
            P("mesh", None),
            P("mesh", None),
            P("mesh", None),
        ),
        out_specs=(P(None, "modes", None, "mesh"), P(None, "modes", None, "mesh")),
        check_vma=False,
    )
```

```python
import functools

import jax
import jax.numpy as jnp
import ml_dtypes
import numpy as np
from jax import lax
from jax.experimental import pallas as pl
from jax.experimental.pallas import tpu as pltpu
from jax.sharding import PartitionSpec as P

COEF = 128
LANES = 128
MESH = pl.DeviceIdType.MESH


highest = lax.Precision.HIGHEST
helm_shift = 4.0
penalty_weight = 200.0
spectral_bound = 400.0
relaxation = 0.8
time_step = 0.02
wave_scale = 0.125
gll_interior = [
    -0.8997579954114602,
    -0.6771862795107377,
    -0.3631174638261782,
    0.0,
    0.3631174638261782,
    0.6771862795107377,
    0.8997579954114602,
]


def shifted(block, axis, distance):
    devices = range(lax.axis_size(axis))
    route = [(i - distance, i) for i in devices if i - distance in devices]
    return lax.ppermute(block, axis, route)


def legendre_value(point, degree):
    previous = 1.0
    current = point
    for order_index in range(1, degree):
        following = ((2 * order_index + 1) * point * current - order_index * previous) / (
            order_index + 1
        )
        previous = current
        current = following
    return current


def spectral_tables(coef_count):
    poly_order = 8
    node_count = poly_order + 1
    points = np.array([-1.0] + gll_interior + [1.0])
    values = np.array([legendre_value(points[node], poly_order) for node in range(node_count)])
    derivative = np.zeros((node_count, node_count))
    for row_index in range(node_count):
        for col_index in range(node_count):
            if row_index != col_index:
                derivative[row_index, col_index] = values[row_index] / (
                    values[col_index] * (points[row_index] - points[col_index])
                )
    derivative[0, 0] = -poly_order * (poly_order + 1) / 4.0
    derivative[poly_order, poly_order] = poly_order * (poly_order + 1) / 4.0
    identity = np.eye(node_count)
    along_r = np.kron(identity, derivative)
    along_s = np.kron(derivative, identity)
    second = np.stack([along_r @ along_r, along_r @ along_s, along_s @ along_s])
    line_nodes = np.arange(node_count)
    edge_nodes = np.stack(
        [
            line_nodes,
            line_nodes * node_count + poly_order,
            poly_order * node_count + line_nodes,
            line_nodes * node_count,
        ]
    )
    counts = np.zeros(node_count * node_count)
    for edge_index in range(4):
        counts[edge_nodes[edge_index]] += 1.0
    planes = np.arange(coef_count) * 2.0 * np.pi / coef_count
    half_count = coef_count // 2
    wavenumber = np.zeros(coef_count)
    basis = np.zeros((coef_count, coef_count))
    z_derivative = np.zeros((coef_count, coef_count))
    basis[:, 0] = 1.0
    basis[:, 1] = np.cos(half_count * planes)
    wavenumber[1] = half_count
    for mode_number in range(1, half_count):
        basis[:, 2 * mode_number] = np.cos(mode_number * planes)
        basis[:, 2 * mode_number + 1] = np.sin(mode_number * planes)
        wavenumber[2 * mode_number] = mode_number
        wavenumber[2 * mode_number + 1] = mode_number
        z_derivative[2 * mode_number, 2 * mode_number + 1] = wave_scale * mode_number
        z_derivative[2 * mode_number + 1, 2 * mode_number] = -wave_scale * mode_number
    norms = np.full(coef_count, coef_count / 2.0)
    norms[0] = coef_count
    norms[1] = coef_count
    inverse = basis.T / norms[:, None]
    shifts = helm_shift + (wave_scale * wavenumber) ** 2
    return along_r, along_s, second, counts, basis, inverse, z_derivative, shifts


def split_table(table):
    exact = np.asarray(table, np.float64).astype(np.float32)
    high = exact.astype(ml_dtypes.bfloat16)
    low = (exact - high.astype(np.float32)).astype(ml_dtypes.bfloat16)
    return high, low


def pad_table(table, rows, cols):
    out = np.zeros((rows, cols))
    out[: table.shape[0], : table.shape[1]] = table
    return out


def split_value(value):
    high = value.astype(jnp.bfloat16)
    low = (value - high.astype(jnp.float32)).astype(jnp.bfloat16)
    return high, low


def mul(a, b):
    return jnp.dot(a, b, preferred_element_type=jnp.float32)


def row_ids():
    return lax.broadcasted_iota(jnp.int32, (8, LANES), 0)


def lane_ids():
    return lax.broadcasted_iota(jnp.int32, (8, LANES), 1)


def lane_take(value, index):
    return jnp.take_along_axis(value, index, axis=1, mode="promise_in_bounds")


def table_row(ref, row):
    return jnp.broadcast_to(ref[row : row + 1, :], (8, LANES))


class Field:
    def __init__(self, ref, part, stride=None):
        self.ref, self.part, self.stride = ref, part, stride

    def rows(self, field, first, count):
        if self.stride is None:
            return self.ref[self.part, field, first : first + count, :]
        start = first * self.stride + field
        if count == 1:
            return self.ref[self.part, pl.ds(start, 1), :]
        return self.ref[self.part, pl.ds(start, count, stride=self.stride), :]

    def spread_row(self, field, row):
        return jnp.broadcast_to(self.rows(field, row, 1), (8, LANES))

    def tile(self, field, tile):
        if tile < 10:
            return self.rows(field, 8 * tile, 8)
        return jnp.where(row_ids() == 0, self.spread_row(field, 80), 0.0)

    def put(self, field, tile, value):
        count = 8 if tile < 10 else 1
        value = value if tile < 10 else value[0:1, :]
        if self.stride is None:
            self.ref[self.part, field, 8 * tile : 8 * tile + count, :] = value
            return
        start = 8 * tile * self.stride + field
        if count == 1:
            self.ref[self.part, pl.ds(start, 1), :] = value
        else:
            self.ref[self.part, pl.ds(start, count, stride=self.stride), :] = value


def swap_groups(planes):
    group = lane_ids() // 8
    planes = list(planes)
    for bit in (1, 2, 4, 8):
        upper = (group & bit) != 0
        for i in range(16):
            if i & bit:
                continue
            j = i | bit
            first, second = planes[i], planes[j]
            planes[i] = jnp.where(upper, pltpu.roll(second, 8 * bit, 1), first)
            planes[j] = jnp.where(upper, second, pltpu.roll(first, LANES - 8 * bit, 1))
    return planes


def emit_halo(source, table_ref, down_ref, up_ref, part, fields):
    pairs = fields // 2
    left = lane_ids() < 64
    for ref, table, base in ((down_ref, 6, 0), (up_ref, 7, 72)):
        index = table_row(table_ref, table)
        for pair in range(pairs):
            a, b = 2 * pair, 2 * pair + 1
            main = jnp.where(
                left,
                lane_take(source.rows(a, base, 8), index),
                lane_take(source.rows(b, base, 8), index),
            )
            ref[part, 8 * pair : 8 * pair + 8, :] = main
            rest = jnp.where(
                left,
                lane_take(source.spread_row(a, base + 8), index),
                lane_take(source.spread_row(b, base + 8), index),
            )
            ref[part, 8 * pairs + pair : 8 * pairs + pair + 1, :] = rest[0:1, :]


def factor_rows(metrics_ref):
    rx, ry, sx, sy = (table_row(metrics_ref, k) for k in range(4))
    return rx * rx + ry * ry, 2.0 * (rx * sx + ry * sy), sx * sx + sy * sy


def halo_kernel(fields, table_ref, x_ref, down_ref, up_ref):
    emit_halo(Field(x_ref, 0, fields), table_ref, down_ref, up_ref, 0, fields)


def apply_operator(fields, operator, source, part, low_ref, top_ref, finish):
    shift_ref, metrics_ref, table_ref, ah_ref, al_ref, diag_ref = operator
    pairs = fields // 2
    start = lax.axis_index("modes") * fields
    fa, fb, fc = factor_rows(metrics_ref)
    base = spectral_bound * (fa + fc) + penalty_weight
    raw = [table_row(table_ref, k) for k in range(6)]
    index = [jnp.maximum(r, 0) for r in raw]
    valid = [r >= 0 for r in raw]
    rows = row_ids()

    def pair_step(pair, carry):
        tiles = [[source.tile(2 * pair + h, t) for t in range(11)] for h in range(2)]
        zero = jnp.zeros((8, LANES), jnp.float32)
        both = jnp.concatenate(
            [jnp.concatenate(tiles[h] + [zero], axis=0) for h in range(2)], axis=1
        )
        high, low = split_value(both)
        ah, al = ah_ref[...], al_ref[...]
        second = mul(ah, high) + (mul(ah, low) + mul(al, high))
        low_main = low_ref[part, pl.ds(pl.multiple_of(8 * pair, 8), 8), :]
        top_main = top_ref[part, pl.ds(pl.multiple_of(8 * pair, 8), 8), :]
        low_rest = jnp.broadcast_to(low_ref[part, pl.ds(8 * pairs + pair, 1), :], (8, LANES))
        top_rest = jnp.broadcast_to(top_ref[part, pl.ds(8 * pairs + pair, 1), :], (8, LANES))
        for h in range(2):
            x = tiles[h]
            field = 2 * pair + h
            shift = shift_ref[start + field]
            scale = relaxation / (base + shift)
            low_index = index[4] + 64 * h
            top_index = index[5] + 64 * h

            def bottom(source, halo):
                own = jnp.where(valid[0], lane_take(source, index[0]), 0.0)
                return jnp.where(valid[4], lane_take(halo, low_index), own)

            def top(source, halo):
                own = jnp.where(valid[2], lane_take(source, index[2]), 0.0)
                return jnp.where(valid[5], lane_take(halo, top_index), own)

            for t in range(11):
                near = zero
                if t > 0 and t != 9:
                    right = jnp.where(valid[1], lane_take(x[t - 1], index[1]), 0.0)
                    near = near + jnp.where((rows + 8 * t) % 9 == 8, right, 0.0)
                if t < 8 or t == 9:
                    left = jnp.where(valid[3], lane_take(x[t + 1], index[3]), 0.0)
                    near = near + jnp.where((rows + 8 * t) % 9 == 0, left, 0.0)
                if t == 0:
                    near = near + bottom(x[9], low_main)
                if t == 1:
                    near = near + jnp.where(rows == 0, bottom(x[10], low_rest), 0.0)
                if t == 9:
                    near = near + top(x[0], top_main)
                if t == 10:
                    near = near + jnp.where(rows == 0, top(x[1], top_rest), 0.0)
                lanes = slice(LANES * h, LANES * h + LANES)
                lap = (
                    fa * second[8 * t : 8 * t + 8, lanes]
                    + fb * second[88 + 8 * t : 96 + 8 * t, lanes]
                    + fc * second[176 + 8 * t : 184 + 8 * t, lanes]
                )
                count = diag_ref[8 * t : 8 * t + 8, :]
                applied = shift * x[t] - lap + penalty_weight * (count * x[t] - near)
                finish(field, t, x[t], applied, scale)
        return carry

    lax.fori_loop(0, pairs, pair_step, 0)


def first_sweep(fields, operator, source, part, low_ref, top_ref, target):
    def finish(field, tile, x, applied, scale):
        target.put(field, tile, x + scale * (helm_shift * x - applied))

    apply_operator(fields, operator, source, part, low_ref, top_ref, finish)


def first_kernel(fields, *refs):
    operator, (x_ref, low_ref, top_ref, out_ref) = refs[:6], refs[6:]
    source, target = Field(x_ref, 0, fields), Field(out_ref, 0)
    first_sweep(fields, operator, source, 0, low_ref, top_ref, target)


def last_kernel(fields, *refs):
    operator = refs[:6]
    x_ref, low_ref, top_ref, vel_ref, adv_ref, out_ref, copy_ref = refs[6:]
    velocity, advection = Field(vel_ref, 0, fields), Field(adv_ref, 0)
    target, copied = Field(out_ref, 0, fields), Field(copy_ref, 0, fields)

    def finish(field, tile, x, applied, scale):
        term = advection.tile(field, tile)
        copied.put(field, tile, term)
        right = helm_shift * (velocity.tile(field, tile) - time_step * term)
        target.put(field, tile, x + scale * (right - applied))

    apply_operator(fields, operator, Field(x_ref, 0), 0, low_ref, top_ref, finish)


def state_kernel(
    fields, shift_ref, metrics_ref, table_ref, adv_ref, part_ref, state_ref, down_ref, up_ref
):
    start = lax.axis_index("modes") * fields
    fa, _, fc = factor_rows(metrics_ref)
    base = spectral_bound * (fa + fc) + penalty_weight
    advection, kept, state = Field(adv_ref, 0), Field(part_ref, 0), Field(state_ref, 0)
    for field in range(fields):
        weight = relaxation * helm_shift * time_step / (base + shift_ref[start + field])
        for tile in range(11):
            value = kept.tile(field, tile) - weight * advection.tile(field, tile)
            state.put(field, tile, value)
    emit_halo(state, table_ref, down_ref, up_ref, 0, fields)


def fused_kernel(
    mesh_count,
    shift_ref,
    metrics_ref,
    table_ref,
    ah_ref,
    al_ref,
    diag_ref,
    scalar_ref,
    bh_ref,
    bl_ref,
    dh_ref,
    dl_ref,
    ih_ref,
    il_ref,
    x_ref,
    state_ref,
    adv_ref,
    low2_ref,
    top2_ref,
    send,
    recv,
    back_send,
    back_recv,
    y0,
    y1,
    y2,
    part_ref,
    down_ref,
    up_ref,
    low_ref,
    top_ref,
    down2_ref,
    up2_ref,
    send_sem,
    recv_sem,
    back_send_sem,
    back_recv_sem,
    halo_send_sem,
    halo_recv_sem,
):
    fields, share = 16, 8
    operator = (shift_ref, metrics_ref, table_ref, ah_ref, al_ref, diag_ref)
    me = lax.axis_index("modes")
    row = lax.axis_index("mesh")
    above = lax.rem(row + 1, mesh_count)
    below = lax.rem(row + mesh_count - 1, mesh_count)
    peers = [lax.rem(me + k, 8) for k in range(8)]
    offset = me * 16
    stages = (y0, y1, y2)
    rows_ref = (below, above) if mesh_count > 1 else ()

    barrier = pltpu.get_barrier_semaphore()
    for k in range(1, 8):
        pl.semaphore_signal(barrier, inc=1, device_id=(row, peers[k]), device_id_type=MESH)
    for other in rows_ref:
        pl.semaphore_signal(barrier, inc=1, device_id=(other, me), device_id_type=MESH)

    def outgoing(half, f, k):
        return pltpu.make_async_remote_copy(
            src_ref=send.at[half, peers[k], pl.ds(88 * f, 88)],
            dst_ref=recv.at[half, me, pl.ds(88 * f, 88)],
            send_sem=send_sem.at[half, f, k],
            recv_sem=recv_sem.at[half, f, k],
            device_id=(row, peers[k]),
            device_id_type=MESH,
        )

    def returning(half, k):
        return pltpu.make_async_remote_copy(
            src_ref=back_send.at[half, peers[k]],
            dst_ref=back_recv.at[half, me],
            send_sem=back_send_sem.at[half, k],
            recv_sem=back_recv_sem.at[half, k],
            device_id=(row, peers[k]),
            device_id_type=MESH,
        )

    def halo_copies(phase, down, up, low, top):
        if mesh_count == 1:
            return []
        return [
            pltpu.make_async_remote_copy(
                src_ref=source,
                dst_ref=target,
                send_sem=halo_send_sem.at[phase, way],
                recv_sem=halo_recv_sem.at[phase, way],
                device_id=(other, me),
                device_id_type=MESH,
            )
            for way, source, target, other in ((0, up, low, above), (1, down, top, below))
        ]

    if mesh_count == 1:
        for ref in (low_ref, top_ref, low2_ref, top2_ref):
            ref[...] = jnp.zeros_like(ref)

    for f in range(3):
        source = Field(x_ref, f, fields)
        for tile in range(11):
            planes = swap_groups([source.tile(c, tile) for c in range(16)])
            first = 88 * f + 8 * tile
            for g in range(16):
                send[g % 2, g // 2, first : first + 8, :] = planes[g]
        if f == 0:
            pl.semaphore_wait(barrier, 7 + len(rows_ref))
        for k in range(1, 8):
            outgoing(0, f, k).start()
    for f in range(3):
        for k in range(1, 8):
            outgoing(1, f, k).start()
    for half in range(2):
        recv[half, me] = send[half, me]
    for f in range(3):
        emit_halo(Field(x_ref, f, fields), table_ref, down_ref, up_ref, f, fields)
    first_halo = halo_copies(0, down_ref, up_ref, low_ref, top_ref)
    for copy in first_halo:
        copy.start()

    for half in range(2):
        for f in range(3):
            for k in range(1, 8):
                outgoing(half, f, k).wait_recv()

        def spread(source, carry):
            for f in range(3):
                part = recv[half, source, 88 * f : 88 * f + 88, :]
                full = jnp.concatenate([part, jnp.zeros((40, LANES), jnp.float32)], axis=0)
                stages[f][pl.ds(pl.multiple_of(source * 128, 128), 128), :] = full.T
            return carry

        lax.fori_loop(0, 8, spread, 0)

        def element(e, carry):
            value = jnp.concatenate(
                [stages[f][pl.ds(e, 128, stride=share), :] for f in range(3)], axis=1
            )
            high, low = split_value(value)
            planes = mul(bh_ref[...], jnp.concatenate([high, low], axis=0)) + mul(
                bl_ref[...], high
            )
            u, v, w = (planes[:128, 128 * f : 128 * f + 128] for f in range(3))
            high, low = split_value(jnp.concatenate([u, v, w], axis=0))
            grads = mul(jnp.concatenate([high, low], axis=1), dh_ref[...]) + mul(
                high, dl_ref[...]
            )
            rx, ry, sx, sy = (scalar_ref[k, offset + share * half + e] for k in range(4))
            along_r = rx * u + ry * v
            along_s = sx * u + sy * v
            terms = []
            for f in range(3):
                rows = slice(128 * f, 128 * f + 128)
                terms.append(
                    along_r * grads[rows, :128]
                    + along_s * grads[rows, 128:]
                    + w * planes[128:, 128 * f : 128 * f + 128]
                )
            high, low = split_value(jnp.concatenate(terms, axis=1))
            back = mul(ih_ref[...], jnp.concatenate([high, low], axis=0)) + mul(
                il_ref[...], high
            )
            for f in range(3):
                stages[f][pl.ds(e, 128, stride=share), :] = back[:, 128 * f : 128 * f + 128]
            return carry

        lax.fori_loop(0, share, element, 0)

        def collect(target, carry):
            for f in range(3):
                full = stages[f][pl.ds(pl.multiple_of(target * 128, 128), 128), :]
                back_send[half, target, 88 * f : 88 * f + 88, :] = full.T[:88, :]
            return carry

        lax.fori_loop(0, 8, collect, 0)
        for k in range(1, 8):
            returning(half, k).start()
        back_recv[half, me] = back_send[half, me]

    for copy in first_halo:
        copy.wait()
    for f in range(3):
        first_sweep(
            fields, operator, Field(x_ref, f, fields), f, low_ref, top_ref, Field(part_ref, f)
        )

    for half in range(2):
        for k in range(1, 8):
            returning(half, k).wait_recv()
    fa, _, fc = factor_rows(metrics_ref)
    base = spectral_bound * (fa + fc) + penalty_weight
    for f in range(3):
        advection, kept, state = Field(adv_ref, f), Field(part_ref, f), Field(state_ref, f)
        for tile in range(11):
            first = 88 * f + 8 * tile
            planes = swap_groups(
                [back_recv[g % 2, g // 2, first : first + 8, :] for g in range(16)]
            )
            for c in range(16):
                advection.put(c, tile, planes[c])
        for c in range(16):
            weight = relaxation * helm_shift * time_step / (base + shift_ref[me * 16 + c])
            for tile in range(11):
                value = kept.tile(c, tile) - weight * advection.tile(c, tile)
                state.put(c, tile, value)
        emit_halo(state, table_ref, down2_ref, up2_ref, f, fields)
    second_halo = halo_copies(1, down2_ref, up2_ref, low2_ref, top2_ref)
    for copy in second_halo:
        copy.start()
    for half in range(2):
        for k in range(1, 8):
            for f in range(3):
                outgoing(half, f, k).wait_send()
            returning(half, k).wait_send()
    for copy in second_halo:
        copy.wait()


def plain_advection(velocity, metrics, tables, mode_count):
    along_r, along_s, basis, inverse, plane_z = tables
    share = velocity.shape[3] // mode_count
    mode_index = lax.axis_index("modes")
    local = lax.dynamic_slice_in_dim(metrics, mode_index * share, share, axis=1)
    field = lax.all_to_all(velocity, "modes", split_axis=3, concat_axis=1, tiled=True)
    physical = jnp.einsum("pc,fcqe->fpqe", basis, field, precision=highest)
    grad_z = jnp.einsum("pc,fcqe->fpqe", plane_z, field, precision=highest)
    grad_r = jnp.einsum("qr,fpre->fpqe", along_r, physical, precision=highest)
    grad_s = jnp.einsum("qr,fpre->fpqe", along_s, physical, precision=highest)
    grad_x = local[0] * grad_r + local[2] * grad_s
    grad_y = local[1] * grad_r + local[3] * grad_s
    term = physical[0] * grad_x + physical[1] * grad_y + physical[2] * grad_z
    spectral = jnp.einsum("cp,fpqe->fcqe", inverse, term, precision=highest)
    return lax.all_to_all(spectral, "modes", split_axis=1, concat_axis=3, tiled=True)


def body(velocity, metrics, connect, send_list, recv_slot):
    along_r, along_s, second, counts, basis, inverse, z_derivative, shifts = spectral_tables(COEF)
    mode_count = lax.axis_size("modes")
    mesh_index = lax.axis_index("mesh")
    fields = velocity.shape[1]
    elements = velocity.shape[3]
    packed = mode_count == 8
    own = jnp.where(
        connect < 0, -1, jnp.clip(connect - mesh_index * elements, 0, elements - 1)
    )
    table = jnp.concatenate(
        [own.T, recv_slot.T, jnp.concatenate([send_list, send_list], axis=1)], axis=0
    )
    shifts = jnp.asarray(shifts, jnp.float32)
    halo_rows = 8 * (fields // 2) + (fields // 2 + 7) // 8 * 8
    ah, al = split_table(
        np.concatenate([pad_table(second[k], 88, 96) for k in range(3)], axis=0)
    )
    diag = np.zeros((88, LANES), np.float32)
    diag[:81] = counts[:, None]

    field_shape = jax.ShapeDtypeStruct(velocity.shape, jnp.float32)
    halo_shape = jax.ShapeDtypeStruct((3, halo_rows, LANES), jnp.float32)
    native = velocity.transpose(0, 2, 1, 3).reshape(3, 81 * fields, LANES)
    native_shape = jax.ShapeDtypeStruct(native.shape, jnp.float32)
    native_spec = pl.BlockSpec((1, 81 * fields, LANES), lambda f: (f, 0, 0))
    field_spec = pl.BlockSpec((1, fields, 81, LANES), lambda f: (f, 0, 0, 0))
    halo_spec = pl.BlockSpec((1, halo_rows, LANES), lambda f: (f, 0, 0))
    smem = pl.BlockSpec(memory_space=pltpu.SMEM)

    def whole(shape):
        return pl.BlockSpec(shape, lambda f: (0,) * len(shape))

    params = pltpu.CompilerParams(vmem_limit_bytes=48 << 20)
    metric_spec, table_spec = whole((4, LANES)), whole((8, LANES))
    operator_specs = [
        smem,
        metric_spec,
        table_spec,
        whole((264, 96)),
        whole((264, 96)),
        whole((88, LANES)),
    ]
    operator_tables = (shifts, metrics, table, jnp.asarray(ah), jnp.asarray(al), jnp.asarray(diag))

    plane_z = basis @ z_derivative
    if packed:
        bh, bl = split_table(np.concatenate([basis, plane_z], axis=0))
        dh, dl = split_table(
            np.concatenate(
                [pad_table(along_r.T, 128, 128), pad_table(along_s.T, 128, 128)], axis=1
            )
        )
        ih, il = split_table(inverse)
        vmem = pl.BlockSpec(memory_space=pltpu.VMEM)
        halo_buffer = pltpu.VMEM((3, halo_rows, LANES), jnp.float32)
        trade_buffer = pltpu.VMEM((2, 8, 264, LANES), jnp.float32)
        state, advection, low, top = pl.pallas_call(
            functools.partial(fused_kernel, lax.axis_size("mesh")),
            in_specs=[smem] + [vmem] * 5 + [smem] + [vmem] * 7,
            out_specs=[vmem] * 4,
            out_shape=[field_shape, field_shape, halo_shape, halo_shape],
            scratch_shapes=[trade_buffer] * 4
            + [pltpu.VMEM((1024, LANES), jnp.float32)] * 3
            + [pltpu.VMEM(velocity.shape, jnp.float32)]
            + [halo_buffer] * 6
            + [pltpu.SemaphoreType.DMA((2, 3, 8))] * 2
            + [pltpu.SemaphoreType.DMA((2, 8))] * 2
            + [pltpu.SemaphoreType.DMA((2, 2))] * 2,
            compiler_params=pltpu.CompilerParams(
                vmem_limit_bytes=48 << 20, collective_id=0, has_side_effects=True
            ),
        )(
            *operator_tables,
            metrics,
            jnp.asarray(np.concatenate([bh, bh], axis=1)),
            jnp.asarray(bl),
            jnp.asarray(np.concatenate([dh, dh], axis=0)),
            jnp.asarray(dl),
            jnp.asarray(np.concatenate([ih, ih], axis=1)),
            jnp.asarray(il),
            native,
        )
    else:
        tables = [
            jnp.asarray(t, jnp.float32) for t in (along_r, along_s, basis, inverse, plane_z)
        ]
        advection = plain_advection(velocity, metrics, tables, mode_count)
        down, up = pl.pallas_call(
            functools.partial(halo_kernel, fields),
            grid=(3,),
            in_specs=[table_spec, native_spec],
            out_specs=[halo_spec, halo_spec],
            out_shape=[halo_shape, halo_shape],
            compiler_params=params,
        )(table, native)
        part = pl.pallas_call(
            functools.partial(first_kernel, fields),
            grid=(3,),
            in_specs=operator_specs + [native_spec, halo_spec, halo_spec],
            out_specs=field_spec,
            out_shape=field_shape,
            compiler_params=params,
        )(*operator_tables, native, shifted(up, "mesh", 1), shifted(down, "mesh", -1))
        state, down, up = pl.pallas_call(
            functools.partial(state_kernel, fields),
            grid=(3,),
            in_specs=[smem, metric_spec, table_spec, field_spec, field_spec],
            out_specs=[field_spec, halo_spec, halo_spec],
            out_shape=[field_shape, halo_shape, halo_shape],
            compiler_params=params,
        )(shifts, metrics, table, advection, part)
        low = shifted(up, "mesh", 1)
        top = shifted(down, "mesh", -1)

    results = pl.pallas_call(
        functools.partial(last_kernel, fields),
        grid=(3,),
        in_specs=operator_specs + [field_spec, halo_spec, halo_spec, native_spec, field_spec],
        out_specs=[native_spec, native_spec],
        out_shape=[native_shape, native_shape],
        compiler_params=params,
    )(*operator_tables, state, low, top, native, advection)
    return tuple(
        out.reshape(3, 81, fields, LANES).transpose(0, 2, 1, 3) for out in results
    )


def solution(mesh):
    return jax.shard_map(
        body,
        mesh=mesh,
        in_specs=(
            P(None, "modes", None, "mesh"),
            P(None, "mesh"),
            P("mesh", None),
            P("mesh", None),
            P("mesh", None),
        ),
        out_specs=(P(None, "modes", None, "mesh"), P(None, "modes", None, "mesh")),
        check_vma=False,
    )
```

```python
import functools

import jax
import jax.numpy as jnp
import ml_dtypes
import numpy as np
from jax import lax
from jax.experimental import pallas as pl
from jax.experimental.pallas import tpu as pltpu
from jax.sharding import PartitionSpec as P

COEF = 128
LANES = 128
MESH = pl.DeviceIdType.MESH


highest = lax.Precision.HIGHEST
helm_shift = 4.0
penalty_weight = 200.0
spectral_bound = 400.0
relaxation = 0.8
time_step = 0.02
wave_scale = 0.125
gll_interior = [
    -0.8997579954114602,
    -0.6771862795107377,
    -0.3631174638261782,
    0.0,
    0.3631174638261782,
    0.6771862795107377,
    0.8997579954114602,
]


def shifted(block, axis, distance):
    devices = range(lax.axis_size(axis))
    route = [(i - distance, i) for i in devices if i - distance in devices]
    return lax.ppermute(block, axis, route)


def legendre_value(point, degree):
    previous = 1.0
    current = point
    for order_index in range(1, degree):
        following = ((2 * order_index + 1) * point * current - order_index * previous) / (
            order_index + 1
        )
        previous = current
        current = following
    return current


def spectral_tables(coef_count):
    poly_order = 8
    node_count = poly_order + 1
    points = np.array([-1.0] + gll_interior + [1.0])
    values = np.array([legendre_value(points[node], poly_order) for node in range(node_count)])
    derivative = np.zeros((node_count, node_count))
    for row_index in range(node_count):
        for col_index in range(node_count):
            if row_index != col_index:
                derivative[row_index, col_index] = values[row_index] / (
                    values[col_index] * (points[row_index] - points[col_index])
                )
    derivative[0, 0] = -poly_order * (poly_order + 1) / 4.0
    derivative[poly_order, poly_order] = poly_order * (poly_order + 1) / 4.0
    identity = np.eye(node_count)
    along_r = np.kron(identity, derivative)
    along_s = np.kron(derivative, identity)
    second = np.stack([along_r @ along_r, along_r @ along_s, along_s @ along_s])
    line_nodes = np.arange(node_count)
    edge_nodes = np.stack(
        [
            line_nodes,
            line_nodes * node_count + poly_order,
            poly_order * node_count + line_nodes,
            line_nodes * node_count,
        ]
    )
    counts = np.zeros(node_count * node_count)
    for edge_index in range(4):
        counts[edge_nodes[edge_index]] += 1.0
    planes = np.arange(coef_count) * 2.0 * np.pi / coef_count
    half_count = coef_count // 2
    wavenumber = np.zeros(coef_count)
    basis = np.zeros((coef_count, coef_count))
    z_derivative = np.zeros((coef_count, coef_count))
    basis[:, 0] = 1.0
    basis[:, 1] = np.cos(half_count * planes)
    wavenumber[1] = half_count
    for mode_number in range(1, half_count):
        basis[:, 2 * mode_number] = np.cos(mode_number * planes)
        basis[:, 2 * mode_number + 1] = np.sin(mode_number * planes)
        wavenumber[2 * mode_number] = mode_number
        wavenumber[2 * mode_number + 1] = mode_number
        z_derivative[2 * mode_number, 2 * mode_number + 1] = wave_scale * mode_number
        z_derivative[2 * mode_number + 1, 2 * mode_number] = -wave_scale * mode_number
    norms = np.full(coef_count, coef_count / 2.0)
    norms[0] = coef_count
    norms[1] = coef_count
    inverse = basis.T / norms[:, None]
    shifts = helm_shift + (wave_scale * wavenumber) ** 2
    return along_r, along_s, second, counts, basis, inverse, z_derivative, shifts


def split_table(table):
    exact = np.asarray(table, np.float64).astype(np.float32)
    high = exact.astype(ml_dtypes.bfloat16)
    low = (exact - high.astype(np.float32)).astype(ml_dtypes.bfloat16)
    return high, low


def pad_table(table, rows, cols):
    out = np.zeros((rows, cols))
    out[: table.shape[0], : table.shape[1]] = table
    return out


def split_value(value):
    high = value.astype(jnp.bfloat16)
    low = (value - high.astype(jnp.float32)).astype(jnp.bfloat16)
    return high, low


def mul(a, b):
    return jnp.dot(a, b, preferred_element_type=jnp.float32)


def row_ids():
    return lax.broadcasted_iota(jnp.int32, (8, LANES), 0)


def lane_ids():
    return lax.broadcasted_iota(jnp.int32, (8, LANES), 1)


def lane_take(value, index):
    return jnp.take_along_axis(value, index, axis=1, mode="promise_in_bounds")


def table_row(ref, row):
    return jnp.broadcast_to(ref[row : row + 1, :], (8, LANES))


class Field:
    def __init__(self, ref, part, stride=None):
        self.ref, self.part, self.stride = ref, part, stride

    def rows(self, field, first, count):
        if self.stride is None:
            return self.ref[self.part, field, first : first + count, :]
        start = first * self.stride + field
        if count == 1:
            return self.ref[self.part, pl.ds(start, 1), :]
        return self.ref[self.part, pl.ds(start, count, stride=self.stride), :]

    def spread_row(self, field, row):
        return jnp.broadcast_to(self.rows(field, row, 1), (8, LANES))

    def tile(self, field, tile):
        if tile < 10:
            return self.rows(field, 8 * tile, 8)
        return jnp.where(row_ids() == 0, self.spread_row(field, 80), 0.0)

    def put(self, field, tile, value):
        count = 8 if tile < 10 else 1
        value = value if tile < 10 else value[0:1, :]
        if self.stride is None:
            self.ref[self.part, field, 8 * tile : 8 * tile + count, :] = value
            return
        start = 8 * tile * self.stride + field
        if count == 1:
            self.ref[self.part, pl.ds(start, 1), :] = value
        else:
            self.ref[self.part, pl.ds(start, count, stride=self.stride), :] = value


def swap_groups(planes):
    group = lane_ids() // 8
    planes = list(planes)
    for bit in (1, 2, 4, 8):
        upper = (group & bit) != 0
        for i in range(16):
            if i & bit:
                continue
            j = i | bit
            first, second = planes[i], planes[j]
            if bit == 8:
                moved = pltpu.roll(jnp.where(upper, first, second), 64, 1)
                planes[i] = jnp.where(upper, moved, first)
                planes[j] = jnp.where(upper, second, moved)
                continue
            planes[i] = jnp.where(upper, pltpu.roll(second, 8 * bit, 1), first)
            planes[j] = jnp.where(upper, second, pltpu.roll(first, LANES - 8 * bit, 1))
    return planes


def emit_halo(source, table_ref, down_ref, up_ref, part, fields):
    pairs = fields // 2
    left = lane_ids() < 64
    for ref, table, base in ((down_ref, 6, 0), (up_ref, 7, 72)):
        index = table_row(table_ref, table)
        for pair in range(pairs):
            a, b = 2 * pair, 2 * pair + 1
            main = jnp.where(
                left,
                lane_take(source.rows(a, base, 8), index),
                lane_take(source.rows(b, base, 8), index),
            )
            ref[part, 8 * pair : 8 * pair + 8, :] = main
            rest = jnp.where(
                left,
                lane_take(source.spread_row(a, base + 8), index),
                lane_take(source.spread_row(b, base + 8), index),
            )
            ref[part, 8 * pairs + pair : 8 * pairs + pair + 1, :] = rest[0:1, :]


def factor_rows(metrics_ref):
    rx, ry, sx, sy = (table_row(metrics_ref, k) for k in range(4))
    return rx * rx + ry * ry, 2.0 * (rx * sx + ry * sy), sx * sx + sy * sy


def halo_kernel(fields, table_ref, x_ref, down_ref, up_ref):
    emit_halo(Field(x_ref, 0, fields), table_ref, down_ref, up_ref, 0, fields)


def apply_operator(fields, operator, source, part, low_ref, top_ref, finish):
    shift_ref, metrics_ref, table_ref, diag_ref, load_second = operator
    pairs = fields // 2
    start = lax.axis_index("modes") * fields
    fa, fb, fc = factor_rows(metrics_ref)
    base = spectral_bound * (fa + fc) + penalty_weight
    raw = [table_row(table_ref, k) for k in range(6)]
    index = [jnp.maximum(r, 0) for r in raw]
    valid = [r >= 0 for r in raw]
    rows = row_ids()

    def pair_step(pair, carry):
        tiles = [[source.tile(2 * pair + h, t) for t in range(11)] for h in range(2)]
        zero = jnp.zeros((8, LANES), jnp.float32)
        both = jnp.concatenate(
            [jnp.concatenate(tiles[h] + [zero], axis=0) for h in range(2)], axis=1
        )
        high, low = split_value(both)
        ah, al = load_second()
        second = mul(ah, high) + (mul(ah, low) + mul(al, high))
        low_main = low_ref[part, pl.ds(pl.multiple_of(8 * pair, 8), 8), :]
        top_main = top_ref[part, pl.ds(pl.multiple_of(8 * pair, 8), 8), :]
        low_rest = jnp.broadcast_to(low_ref[part, pl.ds(8 * pairs + pair, 1), :], (8, LANES))
        top_rest = jnp.broadcast_to(top_ref[part, pl.ds(8 * pairs + pair, 1), :], (8, LANES))
        for h in range(2):
            x = tiles[h]
            field = 2 * pair + h
            shift = shift_ref[start + field]
            scale = relaxation / (base + shift)
            low_index = index[4] + 64 * h
            top_index = index[5] + 64 * h

            def bottom(source, halo):
                own = jnp.where(valid[0], lane_take(source, index[0]), 0.0)
                return jnp.where(valid[4], lane_take(halo, low_index), own)

            def top(source, halo):
                own = jnp.where(valid[2], lane_take(source, index[2]), 0.0)
                return jnp.where(valid[5], lane_take(halo, top_index), own)

            for t in range(11):
                near = zero
                if t > 0 and t != 9:
                    right = jnp.where(valid[1], lane_take(x[t - 1], index[1]), 0.0)
                    near = near + jnp.where(rows == (8 - 8 * t) % 9, right, 0.0)
                if t < 8 or t == 9:
                    left = jnp.where(valid[3], lane_take(x[t + 1], index[3]), 0.0)
                    near = near + jnp.where(rows == -8 * t % 9, left, 0.0)
                if t == 0:
                    near = near + bottom(x[9], low_main)
                if t == 1:
                    near = near + jnp.where(rows == 0, bottom(x[10], low_rest), 0.0)
                if t == 9:
                    near = near + top(x[0], top_main)
                if t == 10:
                    near = near + jnp.where(rows == 0, top(x[1], top_rest), 0.0)
                lanes = slice(LANES * h, LANES * h + LANES)
                lap = (
                    fa * second[8 * t : 8 * t + 8, lanes]
                    + fb * second[88 + 8 * t : 96 + 8 * t, lanes]
                    + fc * second[176 + 8 * t : 184 + 8 * t, lanes]
                )
                count = diag_ref[8 * t : 8 * t + 8, :]
                applied = (shift + count) * x[t] - lap - penalty_weight * near
                finish(field, t, x[t], applied, scale)
        return carry

    lax.fori_loop(0, pairs, pair_step, 0, unroll=2)


def first_sweep(fields, operator, source, part, low_ref, top_ref, target):
    def finish(field, tile, x, applied, scale):
        target.put(field, tile, x + scale * (helm_shift * x - applied))

    apply_operator(fields, operator, source, part, low_ref, top_ref, finish)


def operator_of(refs):
    shift_ref, metrics_ref, table_ref, ah_ref, al_ref, diag_ref = refs
    return shift_ref, metrics_ref, table_ref, diag_ref, lambda: (ah_ref[...], al_ref[...])


def first_kernel(fields, *refs):
    operator, (x_ref, low_ref, top_ref, out_ref) = operator_of(refs[:6]), refs[6:]
    source, target = Field(x_ref, 0, fields), Field(out_ref, 0)
    first_sweep(fields, operator, source, 0, low_ref, top_ref, target)


def last_kernel(fields, *refs):
    operator = operator_of(refs[:6])
    x_ref, low_ref, top_ref, vel_ref, adv_ref, out_ref, copy_ref = refs[6:]
    velocity, advection = Field(vel_ref, 0, fields), Field(adv_ref, 0)
    target, copied = Field(out_ref, 0, fields), Field(copy_ref, 0, fields)

    def finish(field, tile, x, applied, scale):
        term = advection.tile(field, tile)
        copied.put(field, tile, term)
        right = helm_shift * (velocity.tile(field, tile) - time_step * term)
        target.put(field, tile, x + scale * (right - applied))

    apply_operator(fields, operator, Field(x_ref, 0), 0, low_ref, top_ref, finish)


def state_kernel(
    fields, shift_ref, metrics_ref, table_ref, adv_ref, part_ref, state_ref, down_ref, up_ref
):
    start = lax.axis_index("modes") * fields
    fa, _, fc = factor_rows(metrics_ref)
    base = spectral_bound * (fa + fc) + penalty_weight
    advection, kept, state = Field(adv_ref, 0), Field(part_ref, 0), Field(state_ref, 0)
    for field in range(fields):
        weight = relaxation * helm_shift * time_step / (base + shift_ref[start + field])
        for tile in range(11):
            value = kept.tile(field, tile) - weight * advection.tile(field, tile)
            state.put(field, tile, value)
    emit_halo(state, table_ref, down_ref, up_ref, 0, fields)


def fused_kernel(
    mesh_count,
    shift_ref,
    scalar_ref,
    metrics_in,
    connect_in,
    slot_in,
    list_in,
    diag_in,
    constants_in,
    x_in,
    state_ref,
    adv_ref,
    low2_ref,
    top2_ref,
    table_ref,
    metrics_ref,
    connect_ref,
    slot_ref,
    list_ref,
    diag_ref,
    constants,
    x_ref,
    send,
    recv,
    back_send,
    back_recv,
    y0,
    y1,
    y2,
    z0,
    z1,
    z2,
    part_ref,
    down_ref,
    up_ref,
    low_ref,
    top_ref,
    down2_ref,
    up2_ref,
    send_sem,
    recv_sem,
    back_send_sem,
    back_recv_sem,
    halo_send_sem,
    halo_recv_sem,
    load_sem,
):
    fields, share = 16, 8
    operator = (
        shift_ref,
        metrics_ref,
        table_ref,
        diag_ref,
        lambda: (constants[1024:1288, 0:96], constants[1024:1288, 128:224]),
    )
    x_loads = [
        pltpu.make_async_copy(x_in.at[f], x_ref.at[f], load_sem.at[f]) for f in range(3)
    ]
    loads = [
        pltpu.make_async_copy(source, target, load_sem.at[3 + i])
        for i, (source, target) in enumerate(
            (
                (connect_in, connect_ref),
                (slot_in, slot_ref),
                (list_in, list_ref),
                (metrics_in, metrics_ref),
                (diag_in, diag_ref),
                (constants_in, constants),
            )
        )
    ]
    for copy in x_loads + loads:
        copy.start()
    me = lax.axis_index("modes")
    row = lax.axis_index("mesh")
    above = lax.rem(row + 1, mesh_count)
    below = lax.rem(row + mesh_count - 1, mesh_count)
    peers = [lax.rem(me + k, 8) for k in range(8)]
    offset = me * 16
    stages, results = (y0, y1, y2), (z0, z1, z2)
    rows_ref = (below, above) if mesh_count > 1 else ()

    barrier = pltpu.get_barrier_semaphore()
    for k in range(1, 8):
        pl.semaphore_signal(barrier, inc=1, device_id=(row, peers[k]), device_id_type=MESH)
    for other in rows_ref:
        pl.semaphore_signal(barrier, inc=1, device_id=(other, me), device_id_type=MESH)

    def outgoing(half, f, k):
        return pltpu.make_async_remote_copy(
            src_ref=send.at[half, peers[k], pl.ds(88 * f, 88)],
            dst_ref=recv.at[half, me, pl.ds(88 * f, 88)],
            send_sem=send_sem.at[half, f, k],
            recv_sem=recv_sem.at[half, f, k],
            device_id=(row, peers[k]),
            device_id_type=MESH,
        )

    def returning(half, k):
        return pltpu.make_async_remote_copy(
            src_ref=back_send.at[half, peers[k]],
            dst_ref=back_recv.at[half, me],
            send_sem=back_send_sem.at[half, k],
            recv_sem=back_recv_sem.at[half, k],
            device_id=(row, peers[k]),
            device_id_type=MESH,
        )

    def halo_copies(phase, down, up, low, top):
        if mesh_count == 1:
            return []
        return [
            pltpu.make_async_remote_copy(
                src_ref=source,
                dst_ref=target,
                send_sem=halo_send_sem.at[phase, way],
                recv_sem=halo_recv_sem.at[phase, way],
                device_id=(other, me),
                device_id_type=MESH,
            )
            for way, source, target, other in ((0, up, low, above), (1, down, top, below))
        ]

    if mesh_count == 1:
        for ref in (low_ref, top_ref, low2_ref, top2_ref):
            ref[...] = jnp.zeros_like(ref)

    for f in range(3):
        source = Field(x_ref, f, fields)
        x_loads[f].wait()
        for tile in range(11):
            planes = swap_groups([source.tile(c, tile) for c in range(16)])
            first = 88 * f + 8 * tile
            for g in range(16):
                send[g % 2, g // 2, first : first + 8, :] = planes[g]
        if f == 0:
            pl.semaphore_wait(barrier, 7 + len(rows_ref))
        for k in range(1, 8):
            outgoing(0, f, k).start()
    for copy in loads:
        copy.wait()
    elements = connect_ref.shape[1]
    local = jnp.clip(connect_ref[...] - row * elements, 0, elements - 1)
    table_ref[0:4, :] = jnp.where(connect_ref[...] < 0, -1, local)
    table_ref[4:6, :] = slot_ref[...]
    table_ref[6:8, :] = jnp.concatenate([list_ref[...], list_ref[...]], axis=1)
    for f in range(3):
        emit_halo(Field(x_ref, f, fields), table_ref, down_ref, up_ref, f, fields)
    first_halo = halo_copies(0, down_ref, up_ref, low_ref, top_ref)
    for copy in first_halo:
        copy.start()
    for half in range(2):
        recv[half, me] = send[half, me]
    for f in range(3):
        for k in range(1, 8):
            outgoing(1, f, k).start()

    def sweep(f):
        first_sweep(
            fields, operator, Field(x_ref, f, fields), f, low_ref, top_ref, Field(part_ref, f)
        )

    for copy in first_halo:
        copy.wait()
    sweep(0)

    for half in range(2):
        for f in range(3):
            for k in range(1, 8):
                outgoing(half, f, k).wait_recv()

        def spread(source, carry):
            for f in range(3):
                part = recv[half, source, 88 * f : 88 * f + 88, :]
                full = jnp.concatenate([part, jnp.zeros((40, LANES), jnp.float32)], axis=0)
                stages[f][pl.ds(pl.multiple_of(source * 128, 128), 128), :] = full.T
            return carry

        lax.fori_loop(0, 8, spread, 0, unroll=2)

        def element(step, carry):
            picks = (2 * step, 2 * step + 1)
            value = jnp.concatenate(
                [stages[f][pl.ds(e, 128, stride=share), :] for e in picks for f in range(3)],
                axis=1,
            )
            high, low = split_value(value)
            planes = mul(constants[0:256, :], jnp.concatenate([high, low], axis=0)) + mul(
                constants[768:1024, 0:128], high
            )
            parts = [planes[:128, 128 * f : 128 * f + 128] for f in range(6)]
            high, low = split_value(jnp.concatenate(parts, axis=0))
            grads = mul(jnp.concatenate([high, low], axis=1), constants[256:512, :]) + mul(
                high, constants[640:768, :]
            )
            terms = []
            for i, e in enumerate(picks):
                u, v, w = parts[3 * i : 3 * i + 3]
                rx, ry, sx, sy = (scalar_ref[k, offset + share * half + e] for k in range(4))
                along_r = rx * u + ry * v
                along_s = sx * u + sy * v
                for f in range(3 * i, 3 * i + 3):
                    rows = slice(128 * f, 128 * f + 128)
                    terms.append(
                        along_r * grads[rows, :128]
                        + along_s * grads[rows, 128:]
                        + w * planes[128:, 128 * f : 128 * f + 128]
                    )
            high, low = split_value(jnp.concatenate(terms, axis=1))
            back = mul(constants[512:640, :], jnp.concatenate([high, low], axis=0)) + mul(
                constants[768:896, 128:256], high
            )
            for i, e in enumerate(picks):
                for f in range(3):
                    first = 128 * (3 * i + f)
                    results[f][pl.ds(e, 128, stride=share), :] = back[:, first : first + 128]
            return carry

        lax.fori_loop(0, share // 2, element, 0, unroll=2)

        def collect(target, carry):
            for f in range(3):
                full = results[f][pl.ds(pl.multiple_of(target * 128, 128), 128), :]
                back_send[half, target, 88 * f : 88 * f + 88, :] = full.T[:88, :]
            return carry

        lax.fori_loop(0, 8, collect, 0, unroll=2)
        for k in range(1, 8):
            returning(half, k).start()
        back_recv[half, me] = back_send[half, me]

    sweep(1)
    sweep(2)

    for half in range(2):
        for k in range(1, 8):
            returning(half, k).wait_recv()
    fa, _, fc = factor_rows(metrics_ref)
    base = spectral_bound * (fa + fc) + penalty_weight
    for f in range(3):
        advection, kept, state = Field(adv_ref, f), Field(part_ref, f), Field(state_ref, f)
        for tile in range(11):
            first = 88 * f + 8 * tile
            planes = swap_groups(
                [back_recv[g % 2, g // 2, first : first + 8, :] for g in range(16)]
            )
            for c in range(16):
                advection.put(c, tile, planes[c])
        for c in range(16):
            weight = relaxation * helm_shift * time_step / (base + shift_ref[me * 16 + c])
            for tile in range(11):
                value = kept.tile(c, tile) - weight * advection.tile(c, tile)
                state.put(c, tile, value)
        emit_halo(state, table_ref, down2_ref, up2_ref, f, fields)
    second_halo = halo_copies(1, down2_ref, up2_ref, low2_ref, top2_ref)
    for copy in second_halo:
        copy.start()
    for half in range(2):
        for k in range(1, 8):
            for f in range(3):
                outgoing(half, f, k).wait_send()
            returning(half, k).wait_send()
    for copy in second_halo:
        copy.wait()


def plain_advection(velocity, metrics, tables, mode_count):
    along_r, along_s, basis, inverse, plane_z = tables
    share = velocity.shape[3] // mode_count
    mode_index = lax.axis_index("modes")
    local = lax.dynamic_slice_in_dim(metrics, mode_index * share, share, axis=1)
    field = lax.all_to_all(velocity, "modes", split_axis=3, concat_axis=1, tiled=True)
    physical = jnp.einsum("pc,fcqe->fpqe", basis, field, precision=highest)
    grad_z = jnp.einsum("pc,fcqe->fpqe", plane_z, field, precision=highest)
    grad_r = jnp.einsum("qr,fpre->fpqe", along_r, physical, precision=highest)
    grad_s = jnp.einsum("qr,fpre->fpqe", along_s, physical, precision=highest)
    grad_x = local[0] * grad_r + local[2] * grad_s
    grad_y = local[1] * grad_r + local[3] * grad_s
    term = physical[0] * grad_x + physical[1] * grad_y + physical[2] * grad_z
    spectral = jnp.einsum("cp,fpqe->fcqe", inverse, term, precision=highest)
    return lax.all_to_all(spectral, "modes", split_axis=1, concat_axis=3, tiled=True)


def body(velocity, metrics, connect, send_list, recv_slot):
    along_r, along_s, second, counts, basis, inverse, z_derivative, shifts = spectral_tables(COEF)
    mode_count = lax.axis_size("modes")
    mesh_index = lax.axis_index("mesh")
    fields = velocity.shape[1]
    elements = velocity.shape[3]
    packed = mode_count == 8
    shifts = jnp.asarray(shifts, jnp.float32)
    halo_rows = 8 * (fields // 2) + (fields // 2 + 7) // 8 * 8
    ah, al = split_table(
        np.concatenate([pad_table(second[k], 88, 96) for k in range(3)], axis=0)
    )
    diag = np.zeros((88, LANES), np.float32)
    diag[:81] = penalty_weight * counts[:, None]

    field_shape = jax.ShapeDtypeStruct(velocity.shape, jnp.float32)
    halo_shape = jax.ShapeDtypeStruct((3, halo_rows, LANES), jnp.float32)
    native = velocity.transpose(0, 2, 1, 3).reshape(3, 81 * fields, LANES)
    native_shape = jax.ShapeDtypeStruct(native.shape, jnp.float32)
    native_spec = pl.BlockSpec((1, 81 * fields, LANES), lambda f: (f, 0, 0))
    field_spec = pl.BlockSpec((1, fields, 81, LANES), lambda f: (f, 0, 0, 0))
    halo_spec = pl.BlockSpec((1, halo_rows, LANES), lambda f: (f, 0, 0))
    smem = pl.BlockSpec(memory_space=pltpu.SMEM)

    def whole(shape):
        return pl.BlockSpec(shape, lambda f: (0,) * len(shape))

    params = pltpu.CompilerParams(vmem_limit_bytes=60 << 20)
    metric_spec, table_spec = whole((4, LANES)), whole((8, LANES))
    operator_specs = [
        smem,
        metric_spec,
        table_spec,
        whole((264, 96)),
        whole((264, 96)),
        whole((88, LANES)),
    ]
    ah_table, al_table, diag_table = (jnp.asarray(t) for t in (ah, al, diag))

    plane_z = basis @ z_derivative
    if packed:
        bh, bl = split_table(np.concatenate([basis, plane_z], axis=0))
        dh, dl = split_table(
            np.concatenate(
                [pad_table(along_r.T, 128, 128), pad_table(along_s.T, 128, 128)], axis=1
            )
        )
        ih, il = split_table(inverse)
        constants = np.zeros((1296, 256), ml_dtypes.bfloat16)
        constants[0:256] = np.concatenate([bh, bh], axis=1)
        constants[256:512] = np.concatenate([dh, dh], axis=0)
        constants[512:640] = np.concatenate([ih, ih], axis=1)
        constants[640:768] = dl
        constants[768:1024, 0:128] = bl
        constants[768:896, 128:256] = il
        constants[1024:1288, 0:96] = ah
        constants[1024:1288, 128:224] = al
        vmem = pl.BlockSpec(memory_space=pltpu.VMEM)
        hbm = pl.BlockSpec(memory_space=pltpu.HBM)
        halo_buffer = pltpu.VMEM((3, halo_rows, LANES), jnp.float32)
        trade_buffer = pltpu.VMEM((2, 8, 264, LANES), jnp.float32)
        state, advection, low, top, table = pl.pallas_call(
            functools.partial(fused_kernel, lax.axis_size("mesh")),
            in_specs=[smem] * 2 + [hbm] * 7,
            out_specs=[vmem] * 5,
            out_shape=[
                field_shape,
                field_shape,
                halo_shape,
                halo_shape,
                jax.ShapeDtypeStruct((8, LANES), jnp.int32),
            ],
            scratch_shapes=[
                pltpu.VMEM((4, LANES), jnp.float32),
                pltpu.VMEM((4, LANES), jnp.int32),
                pltpu.VMEM((2, LANES), jnp.int32),
                pltpu.VMEM(send_list.shape, jnp.int32),
                pltpu.VMEM(diag.shape, jnp.float32),
                pltpu.VMEM(constants.shape, jnp.bfloat16),
                pltpu.VMEM(native.shape, jnp.float32),
            ]
            + [trade_buffer] * 4
            + [pltpu.VMEM((1024, LANES), jnp.float32)] * 6
            + [pltpu.VMEM(velocity.shape, jnp.float32)]
            + [halo_buffer] * 6
            + [pltpu.SemaphoreType.DMA((2, 3, 8))] * 2
            + [pltpu.SemaphoreType.DMA((2, 8))] * 2
            + [pltpu.SemaphoreType.DMA((2, 2))] * 2
            + [pltpu.SemaphoreType.DMA((9,))],
            compiler_params=pltpu.CompilerParams(
                vmem_limit_bytes=60 << 20, collective_id=0, has_side_effects=True
            ),
        )(
            shifts,
            metrics,
            metrics,
            connect.T,
            recv_slot.T,
            send_list,
            jnp.asarray(diag),
            jnp.asarray(constants),
            native,
        )
    else:
        own = jnp.where(
            connect < 0, -1, jnp.clip(connect - mesh_index * elements, 0, elements - 1)
        )
        table = jnp.concatenate(
            [own.T, recv_slot.T, jnp.concatenate([send_list, send_list], axis=1)], axis=0
        )
        tables = [
            jnp.asarray(t, jnp.float32) for t in (along_r, along_s, basis, inverse, plane_z)
        ]
        advection = plain_advection(velocity, metrics, tables, mode_count)
        down, up = pl.pallas_call(
            functools.partial(halo_kernel, fields),
            grid=(3,),
            in_specs=[table_spec, native_spec],
            out_specs=[halo_spec, halo_spec],
            out_shape=[halo_shape, halo_shape],
            compiler_params=params,
        )(table, native)
        part = pl.pallas_call(
            functools.partial(first_kernel, fields),
            grid=(3,),
            in_specs=operator_specs + [native_spec, halo_spec, halo_spec],
            out_specs=field_spec,
            out_shape=field_shape,
            compiler_params=params,
        )(shifts, metrics, table, ah_table, al_table, diag_table, native, shifted(up, "mesh", 1), shifted(down, "mesh", -1))
        state, down, up = pl.pallas_call(
            functools.partial(state_kernel, fields),
            grid=(3,),
            in_specs=[smem, metric_spec, table_spec, field_spec, field_spec],
            out_specs=[field_spec, halo_spec, halo_spec],
            out_shape=[field_shape, halo_shape, halo_shape],
            compiler_params=params,
        )(shifts, metrics, table, advection, part)
        low = shifted(up, "mesh", 1)
        top = shifted(down, "mesh", -1)

    results = pl.pallas_call(
        functools.partial(last_kernel, fields),
        grid=(3,),
        in_specs=operator_specs + [field_spec, halo_spec, halo_spec, native_spec, field_spec],
        out_specs=[native_spec, native_spec],
        out_shape=[native_shape, native_shape],
        compiler_params=params,
    )(shifts, metrics, table, ah_table, al_table, diag_table, state, low, top, native, advection)
    return tuple(
        out.reshape(3, 81, fields, LANES).transpose(0, 2, 1, 3) for out in results
    )


def solution(mesh):
    return jax.shard_map(
        body,
        mesh=mesh,
        in_specs=(
            P(None, "modes", None, "mesh"),
            P(None, "mesh"),
            P("mesh", None),
            P("mesh", None),
            P("mesh", None),
        ),
        out_specs=(P(None, "modes", None, "mesh"), P(None, "modes", None, "mesh")),
        check_vma=False,
    )
```

```python
import functools

import jax
import jax.numpy as jnp
import ml_dtypes
import numpy as np
from jax import lax
from jax.experimental import pallas as pl
from jax.experimental.pallas import tpu as pltpu
from jax.sharding import PartitionSpec as P

COEF = 128
LANES = 128
MESH = pl.DeviceIdType.MESH


highest = lax.Precision.HIGHEST
helm_shift = 4.0
penalty_weight = 200.0
spectral_bound = 400.0
relaxation = 0.8
time_step = 0.02
wave_scale = 0.125
gll_interior = [
    -0.8997579954114602,
    -0.6771862795107377,
    -0.3631174638261782,
    0.0,
    0.3631174638261782,
    0.6771862795107377,
    0.8997579954114602,
]


def shifted(block, axis, distance):
    devices = range(lax.axis_size(axis))
    route = [(i - distance, i) for i in devices if i - distance in devices]
    return lax.ppermute(block, axis, route)


def legendre_value(point, degree):
    previous = 1.0
    current = point
    for order_index in range(1, degree):
        following = ((2 * order_index + 1) * point * current - order_index * previous) / (
            order_index + 1
        )
        previous = current
        current = following
    return current


def spectral_tables(coef_count):
    poly_order = 8
    node_count = poly_order + 1
    points = np.array([-1.0] + gll_interior + [1.0])
    values = np.array([legendre_value(points[node], poly_order) for node in range(node_count)])
    derivative = np.zeros((node_count, node_count))
    for row_index in range(node_count):
        for col_index in range(node_count):
            if row_index != col_index:
                derivative[row_index, col_index] = values[row_index] / (
                    values[col_index] * (points[row_index] - points[col_index])
                )
    derivative[0, 0] = -poly_order * (poly_order + 1) / 4.0
    derivative[poly_order, poly_order] = poly_order * (poly_order + 1) / 4.0
    identity = np.eye(node_count)
    along_r = np.kron(identity, derivative)
    along_s = np.kron(derivative, identity)
    second = np.stack([along_r @ along_r, along_r @ along_s, along_s @ along_s])
    line_nodes = np.arange(node_count)
    edge_nodes = np.stack(
        [
            line_nodes,
            line_nodes * node_count + poly_order,
            poly_order * node_count + line_nodes,
            line_nodes * node_count,
        ]
    )
    counts = np.zeros(node_count * node_count)
    for edge_index in range(4):
        counts[edge_nodes[edge_index]] += 1.0
    planes = np.arange(coef_count) * 2.0 * np.pi / coef_count
    half_count = coef_count // 2
    wavenumber = np.zeros(coef_count)
    basis = np.zeros((coef_count, coef_count))
    z_derivative = np.zeros((coef_count, coef_count))
    basis[:, 0] = 1.0
    basis[:, 1] = np.cos(half_count * planes)
    wavenumber[1] = half_count
    for mode_number in range(1, half_count):
        basis[:, 2 * mode_number] = np.cos(mode_number * planes)
        basis[:, 2 * mode_number + 1] = np.sin(mode_number * planes)
        wavenumber[2 * mode_number] = mode_number
        wavenumber[2 * mode_number + 1] = mode_number
        z_derivative[2 * mode_number, 2 * mode_number + 1] = wave_scale * mode_number
        z_derivative[2 * mode_number + 1, 2 * mode_number] = -wave_scale * mode_number
    norms = np.full(coef_count, coef_count / 2.0)
    norms[0] = coef_count
    norms[1] = coef_count
    inverse = basis.T / norms[:, None]
    shifts = helm_shift + (wave_scale * wavenumber) ** 2
    return along_r, along_s, second, counts, basis, inverse, z_derivative, shifts


def split_table(table):
    exact = np.asarray(table, np.float64).astype(np.float32)
    high = exact.astype(ml_dtypes.bfloat16)
    low = (exact - high.astype(np.float32)).astype(ml_dtypes.bfloat16)
    return high, low


def pad_table(table, rows, cols):
    out = np.zeros((rows, cols))
    out[: table.shape[0], : table.shape[1]] = table
    return out


def split_value(value):
    high = value.astype(jnp.bfloat16)
    low = (value - high.astype(jnp.float32)).astype(jnp.bfloat16)
    return high, low


def mul(a, b):
    return jnp.dot(a, b, preferred_element_type=jnp.float32)


def row_ids():
    return lax.broadcasted_iota(jnp.int32, (8, LANES), 0)


def lane_ids():
    return lax.broadcasted_iota(jnp.int32, (8, LANES), 1)


def lane_take(value, index):
    return jnp.take_along_axis(value, index, axis=1, mode="promise_in_bounds")


def table_row(ref, row):
    return jnp.broadcast_to(ref[row : row + 1, :], (8, LANES))


class Field:
    def __init__(self, ref, part, stride=None):
        self.ref, self.part, self.stride = ref, part, stride

    def rows(self, field, first, count):
        if self.stride is None:
            return self.ref[self.part, field, first : first + count, :]
        start = first * self.stride + field
        if count == 1:
            return self.ref[self.part, pl.ds(start, 1), :]
        return self.ref[self.part, pl.ds(start, count, stride=self.stride), :]

    def spread_row(self, field, row):
        return jnp.broadcast_to(self.rows(field, row, 1), (8, LANES))

    def tile(self, field, tile):
        if tile < 10:
            return self.rows(field, 8 * tile, 8)
        return jnp.where(row_ids() == 0, self.spread_row(field, 80), 0.0)

    def put(self, field, tile, value):
        count = 8 if tile < 10 else 1
        value = value if tile < 10 else value[0:1, :]
        if self.stride is None:
            self.ref[self.part, field, 8 * tile : 8 * tile + count, :] = value
            return
        start = 8 * tile * self.stride + field
        if count == 1:
            self.ref[self.part, pl.ds(start, 1), :] = value
        else:
            self.ref[self.part, pl.ds(start, count, stride=self.stride), :] = value


def swap_groups(planes):
    group = lane_ids() // 8
    planes = list(planes)
    for bit in (1, 2, 4, 8):
        upper = (group & bit) != 0
        for i in range(16):
            if i & bit:
                continue
            j = i | bit
            first, second = planes[i], planes[j]
            if bit == 8:
                moved = pltpu.roll(jnp.where(upper, first, second), 64, 1)
                planes[i] = jnp.where(upper, moved, first)
                planes[j] = jnp.where(upper, second, moved)
                continue
            planes[i] = jnp.where(upper, pltpu.roll(second, 8 * bit, 1), first)
            planes[j] = jnp.where(upper, second, pltpu.roll(first, LANES - 8 * bit, 1))
    return planes


def emit_halo(source, table_ref, down_ref, up_ref, part, fields):
    pairs = fields // 2
    left = lane_ids() < 64
    for ref, table, base in ((down_ref, 6, 0), (up_ref, 7, 72)):
        index = table_row(table_ref, table)
        for pair in range(pairs):
            a, b = 2 * pair, 2 * pair + 1
            main = jnp.where(
                left,
                lane_take(source.rows(a, base, 8), index),
                lane_take(source.rows(b, base, 8), index),
            )
            ref[part, 8 * pair : 8 * pair + 8, :] = main
            rest = jnp.where(
                left,
                lane_take(source.spread_row(a, base + 8), index),
                lane_take(source.spread_row(b, base + 8), index),
            )
            ref[part, 8 * pairs + pair : 8 * pairs + pair + 1, :] = rest[0:1, :]


def factor_rows(metrics_ref):
    rx, ry, sx, sy = (table_row(metrics_ref, k) for k in range(4))
    return rx * rx + ry * ry, 2.0 * (rx * sx + ry * sy), sx * sx + sy * sy


def halo_kernel(fields, table_ref, x_ref, down_ref, up_ref):
    emit_halo(Field(x_ref, 0, fields), table_ref, down_ref, up_ref, 0, fields)


def apply_operator(fields, operator, source, part, low_ref, top_ref, finish):
    shift_ref, metrics_ref, table_ref, diag_ref, load_second = operator
    pairs = fields // 2
    start = lax.axis_index("modes") * fields
    fa, fb, fc = factor_rows(metrics_ref)
    base = spectral_bound * (fa + fc) + penalty_weight
    raw = [table_row(table_ref, k) for k in range(6)]
    index = [jnp.maximum(r, 0) for r in raw]
    valid = [r >= 0 for r in raw]
    rows = row_ids()

    def pair_step(pair, carry):
        tiles = [[source.tile(2 * pair + h, t) for t in range(11)] for h in range(2)]
        zero = jnp.zeros((8, LANES), jnp.float32)
        both = jnp.concatenate(
            [jnp.concatenate(tiles[h] + [zero], axis=0) for h in range(2)], axis=1
        )
        high, low = split_value(both)
        ah, al = load_second()
        second = mul(ah, high) + (mul(ah, low) + mul(al, high))
        low_main = low_ref[part, pl.ds(pl.multiple_of(8 * pair, 8), 8), :]
        top_main = top_ref[part, pl.ds(pl.multiple_of(8 * pair, 8), 8), :]
        low_rest = jnp.broadcast_to(low_ref[part, pl.ds(8 * pairs + pair, 1), :], (8, LANES))
        top_rest = jnp.broadcast_to(top_ref[part, pl.ds(8 * pairs + pair, 1), :], (8, LANES))
        for h in range(2):
            x = tiles[h]
            field = 2 * pair + h
            shift = shift_ref[start + field]
            scale = relaxation / (base + shift)
            low_index = index[4] + 64 * h
            top_index = index[5] + 64 * h

            def bottom(source, halo):
                own = jnp.where(valid[0], lane_take(source, index[0]), 0.0)
                return jnp.where(valid[4], lane_take(halo, low_index), own)

            def top(source, halo):
                own = jnp.where(valid[2], lane_take(source, index[2]), 0.0)
                return jnp.where(valid[5], lane_take(halo, top_index), own)

            for t in range(11):
                near = zero
                if t > 0 and t != 9:
                    right = jnp.where(valid[1], lane_take(x[t - 1], index[1]), 0.0)
                    near = near + jnp.where(rows == (8 - 8 * t) % 9, right, 0.0)
                if t < 8 or t == 9:
                    left = jnp.where(valid[3], lane_take(x[t + 1], index[3]), 0.0)
                    near = near + jnp.where(rows == -8 * t % 9, left, 0.0)
                if t == 0:
                    near = near + bottom(x[9], low_main)
                if t == 1:
                    near = near + jnp.where(rows == 0, bottom(x[10], low_rest), 0.0)
                if t == 9:
                    near = near + top(x[0], top_main)
                if t == 10:
                    near = near + jnp.where(rows == 0, top(x[1], top_rest), 0.0)
                lanes = slice(LANES * h, LANES * h + LANES)
                lap = (
                    fa * second[8 * t : 8 * t + 8, lanes]
                    + fb * second[88 + 8 * t : 96 + 8 * t, lanes]
                    + fc * second[176 + 8 * t : 184 + 8 * t, lanes]
                )
                count = diag_ref[8 * t : 8 * t + 8, :]
                applied = (shift + count) * x[t] - lap - penalty_weight * near
                finish(field, t, x[t], applied, scale)
        return carry

    lax.fori_loop(0, pairs, pair_step, 0, unroll=2)


def first_sweep(fields, operator, source, part, low_ref, top_ref, target):
    def finish(field, tile, x, applied, scale):
        target.put(field, tile, x + scale * (helm_shift * x - applied))

    apply_operator(fields, operator, source, part, low_ref, top_ref, finish)


def operator_of(refs):
    shift_ref, metrics_ref, table_ref, ah_ref, al_ref, diag_ref = refs
    return shift_ref, metrics_ref, table_ref, diag_ref, lambda: (ah_ref[...], al_ref[...])


def first_kernel(fields, *refs):
    operator, (x_ref, low_ref, top_ref, out_ref) = operator_of(refs[:6]), refs[6:]
    source, target = Field(x_ref, 0, fields), Field(out_ref, 0)
    first_sweep(fields, operator, source, 0, low_ref, top_ref, target)


def last_kernel(fields, *refs):
    operator = operator_of(refs[:6])
    x_ref, low_ref, top_ref, vel_ref, adv_ref, out_ref, copy_ref = refs[6:]
    velocity, advection = Field(vel_ref, 0, fields), Field(adv_ref, 0)
    target, copied = Field(out_ref, 0, fields), Field(copy_ref, 0, fields)

    def finish(field, tile, x, applied, scale):
        term = advection.tile(field, tile)
        copied.put(field, tile, term)
        right = helm_shift * (velocity.tile(field, tile) - time_step * term)
        target.put(field, tile, x + scale * (right - applied))

    apply_operator(fields, operator, Field(x_ref, 0), 0, low_ref, top_ref, finish)


def state_kernel(
    fields, shift_ref, metrics_ref, table_ref, adv_ref, part_ref, state_ref, down_ref, up_ref
):
    start = lax.axis_index("modes") * fields
    fa, _, fc = factor_rows(metrics_ref)
    base = spectral_bound * (fa + fc) + penalty_weight
    advection, kept, state = Field(adv_ref, 0), Field(part_ref, 0), Field(state_ref, 0)
    for field in range(fields):
        weight = relaxation * helm_shift * time_step / (base + shift_ref[start + field])
        for tile in range(11):
            value = kept.tile(field, tile) - weight * advection.tile(field, tile)
            state.put(field, tile, value)
    emit_halo(state, table_ref, down_ref, up_ref, 0, fields)


def fused_kernel(
    mesh_count,
    shift_ref,
    scalar_ref,
    metrics_in,
    connect_in,
    slot_in,
    list_in,
    diag_in,
    constants_in,
    x_in,
    state_ref,
    adv_ref,
    low2_ref,
    top2_ref,
    table_ref,
    metrics_ref,
    connect_ref,
    slot_ref,
    list_ref,
    diag_ref,
    constants,
    x_ref,
    send,
    recv,
    back_send,
    back_recv,
    y0,
    y1,
    y2,
    z0,
    z1,
    z2,
    part_ref,
    down_ref,
    up_ref,
    low_ref,
    top_ref,
    down2_ref,
    up2_ref,
    send_sem,
    recv_sem,
    back_send_sem,
    back_recv_sem,
    halo_send_sem,
    halo_recv_sem,
    load_sem,
):
    fields, share = 16, 8
    operator = (
        shift_ref,
        metrics_ref,
        table_ref,
        diag_ref,
        lambda: (constants[1024:1288, 0:96], constants[1024:1288, 128:224]),
    )
    x_loads = [
        pltpu.make_async_copy(x_in.at[f], x_ref.at[f], load_sem.at[f]) for f in range(3)
    ]
    loads = [
        pltpu.make_async_copy(source, target, load_sem.at[3 + i])
        for i, (source, target) in enumerate(
            (
                (connect_in, connect_ref),
                (slot_in, slot_ref),
                (list_in, list_ref),
                (metrics_in, metrics_ref),
                (diag_in, diag_ref),
                (constants_in, constants),
            )
        )
    ]
    for copy in x_loads + loads:
        copy.start()
    me = lax.axis_index("modes")
    row = lax.axis_index("mesh")
    above = lax.rem(row + 1, mesh_count)
    below = lax.rem(row + mesh_count - 1, mesh_count)
    peers = [lax.rem(me + k, 8) for k in range(8)]
    offset = me * 16
    stages, results = (y0, y1, y2), (z0, z1, z2)
    rows_ref = (below, above) if mesh_count > 1 else ()

    barrier = pltpu.get_barrier_semaphore()
    for k in range(1, 8):
        pl.semaphore_signal(barrier, inc=1, device_id=(row, peers[k]), device_id_type=MESH)
    for other in rows_ref:
        pl.semaphore_signal(barrier, inc=1, device_id=(other, me), device_id_type=MESH)

    def outgoing(half, f, k):
        return pltpu.make_async_remote_copy(
            src_ref=send.at[half, peers[k], pl.ds(88 * f, 88)],
            dst_ref=recv.at[half, me, pl.ds(88 * f, 88)],
            send_sem=send_sem.at[half, f, k],
            recv_sem=recv_sem.at[half, f, k],
            device_id=(row, peers[k]),
            device_id_type=MESH,
        )

    def returning(half, f, k):
        return pltpu.make_async_remote_copy(
            src_ref=back_send.at[half, peers[k], pl.ds(88 * f, 88)],
            dst_ref=back_recv.at[half, me, pl.ds(88 * f, 88)],
            send_sem=back_send_sem.at[half, f, k],
            recv_sem=back_recv_sem.at[half, f, k],
            device_id=(row, peers[k]),
            device_id_type=MESH,
        )

    def halo_copies(phase, down, up, low, top):
        if mesh_count == 1:
            return []
        return [
            pltpu.make_async_remote_copy(
                src_ref=source,
                dst_ref=target,
                send_sem=halo_send_sem.at[phase, way],
                recv_sem=halo_recv_sem.at[phase, way],
                device_id=(other, me),
                device_id_type=MESH,
            )
            for way, source, target, other in ((0, up, low, above), (1, down, top, below))
        ]

    if mesh_count == 1:
        for ref in (low_ref, top_ref, low2_ref, top2_ref):
            ref[...] = jnp.zeros_like(ref)

    for f in range(3):
        source = Field(x_ref, f, fields)
        x_loads[f].wait()
        for tile in range(11):
            planes = swap_groups([source.tile(c, tile) for c in range(16)])
            first = 88 * f + 8 * tile
            for g in range(16):
                send[g % 2, g // 2, first : first + 8, :] = planes[g]
        if f == 0:
            pl.semaphore_wait(barrier, 7 + len(rows_ref))
        for k in range(1, 8):
            outgoing(0, f, k).start()
    for copy in loads:
        copy.wait()
    elements = connect_ref.shape[1]
    local = jnp.clip(connect_ref[...] - row * elements, 0, elements - 1)
    table_ref[0:4, :] = jnp.where(connect_ref[...] < 0, -1, local)
    table_ref[4:6, :] = slot_ref[...]
    table_ref[6:8, :] = jnp.concatenate([list_ref[...], list_ref[...]], axis=1)
    for f in range(3):
        emit_halo(Field(x_ref, f, fields), table_ref, down_ref, up_ref, f, fields)
    first_halo = halo_copies(0, down_ref, up_ref, low_ref, top_ref)
    for copy in first_halo:
        copy.start()
    for half in range(2):
        recv[half, me] = send[half, me]
    for f in range(3):
        for k in range(1, 8):
            outgoing(1, f, k).start()

    def sweep(f):
        first_sweep(
            fields, operator, Field(x_ref, f, fields), f, low_ref, top_ref, Field(part_ref, f)
        )

    for copy in first_halo:
        copy.wait()
    sweep(0)

    for half in range(2):
        for f in range(3):
            for k in range(1, 8):
                outgoing(half, f, k).wait_recv()

        def spread(source, carry):
            for f in range(3):
                part = recv[half, source, 88 * f : 88 * f + 88, :]
                full = jnp.concatenate([part, jnp.zeros((40, LANES), jnp.float32)], axis=0)
                stages[f][pl.ds(pl.multiple_of(source * 128, 128), 128), :] = full.T
            return carry

        lax.fori_loop(0, 8, spread, 0, unroll=2)

        def element(step, carry):
            picks = (2 * step, 2 * step + 1)
            value = jnp.concatenate(
                [stages[f][pl.ds(e, 128, stride=share), :] for e in picks for f in range(3)],
                axis=1,
            )
            high, low = split_value(value)
            planes = mul(constants[0:256, :], jnp.concatenate([high, low], axis=0)) + mul(
                constants[768:1024, 0:128], high
            )
            parts = [planes[:128, 128 * f : 128 * f + 128] for f in range(6)]
            high, low = split_value(jnp.concatenate(parts, axis=0))
            grads = mul(jnp.concatenate([high, low], axis=1), constants[256:512, :]) + mul(
                high, constants[640:768, :]
            )
            terms = []
            for i, e in enumerate(picks):
                u, v, w = parts[3 * i : 3 * i + 3]
                rx, ry, sx, sy = (scalar_ref[k, offset + share * half + e] for k in range(4))
                along_r = rx * u + ry * v
                along_s = sx * u + sy * v
                for f in range(3 * i, 3 * i + 3):
                    rows = slice(128 * f, 128 * f + 128)
                    terms.append(
                        along_r * grads[rows, :128]
                        + along_s * grads[rows, 128:]
                        + w * planes[128:, 128 * f : 128 * f + 128]
                    )
            high, low = split_value(jnp.concatenate(terms, axis=1))
            back = mul(constants[512:640, :], jnp.concatenate([high, low], axis=0)) + mul(
                constants[768:896, 128:256], high
            )
            for i, e in enumerate(picks):
                for f in range(3):
                    first = 128 * (3 * i + f)
                    results[f][pl.ds(e, 128, stride=share), :] = back[:, first : first + 128]
            return carry

        lax.fori_loop(0, share // 2, element, 0, unroll=2)

        def collect(target, carry):
            for f in range(3):
                full = results[f][pl.ds(pl.multiple_of(target * 128, 128), 128), :]
                back_send[half, target, 88 * f : 88 * f + 88, :] = full.T[:88, :]
            return carry

        lax.fori_loop(0, 8, collect, 0, unroll=2)
        for f in range(3):
            for k in range(1, 8):
                returning(half, f, k).start()
        back_recv[half, me] = back_send[half, me]

    sweep(1)
    sweep(2)

    fa, _, fc = factor_rows(metrics_ref)
    base = spectral_bound * (fa + fc) + penalty_weight
    second_halo = []
    for f in range(3):
        advection, kept, state = Field(adv_ref, f), Field(part_ref, f), Field(state_ref, f)
        for half in range(2):
            for k in range(1, 8):
                returning(half, f, k).wait_recv()
        for tile in range(11):
            first = 88 * f + 8 * tile
            planes = swap_groups(
                [back_recv[g % 2, g // 2, first : first + 8, :] for g in range(16)]
            )
            for c in range(16):
                advection.put(c, tile, planes[c])
        for c in range(16):
            weight = relaxation * helm_shift * time_step / (base + shift_ref[me * 16 + c])
            for tile in range(11):
                value = kept.tile(c, tile) - weight * advection.tile(c, tile)
                state.put(c, tile, value)
        emit_halo(state, table_ref, down2_ref, up2_ref, f, fields)
        copies = halo_copies(
            1 + f, down2_ref.at[f], up2_ref.at[f], low2_ref.at[f], top2_ref.at[f]
        )
        for copy in copies:
            copy.start()
        second_halo.extend(copies)
    for half in range(2):
        for k in range(1, 8):
            for f in range(3):
                outgoing(half, f, k).wait_send()
                returning(half, f, k).wait_send()
    for copy in second_halo:
        copy.wait()


def plain_advection(velocity, metrics, tables, mode_count):
    along_r, along_s, basis, inverse, plane_z = tables
    share = velocity.shape[3] // mode_count
    mode_index = lax.axis_index("modes")
    local = lax.dynamic_slice_in_dim(metrics, mode_index * share, share, axis=1)
    field = lax.all_to_all(velocity, "modes", split_axis=3, concat_axis=1, tiled=True)
    physical = jnp.einsum("pc,fcqe->fpqe", basis, field, precision=highest)
    grad_z = jnp.einsum("pc,fcqe->fpqe", plane_z, field, precision=highest)
    grad_r = jnp.einsum("qr,fpre->fpqe", along_r, physical, precision=highest)
    grad_s = jnp.einsum("qr,fpre->fpqe", along_s, physical, precision=highest)
    grad_x = local[0] * grad_r + local[2] * grad_s
    grad_y = local[1] * grad_r + local[3] * grad_s
    term = physical[0] * grad_x + physical[1] * grad_y + physical[2] * grad_z
    spectral = jnp.einsum("cp,fpqe->fcqe", inverse, term, precision=highest)
    return lax.all_to_all(spectral, "modes", split_axis=1, concat_axis=3, tiled=True)


def body(velocity, metrics, connect, send_list, recv_slot):
    along_r, along_s, second, counts, basis, inverse, z_derivative, shifts = spectral_tables(COEF)
    mode_count = lax.axis_size("modes")
    mesh_index = lax.axis_index("mesh")
    fields = velocity.shape[1]
    elements = velocity.shape[3]
    packed = mode_count == 8
    shifts = jnp.asarray(shifts, jnp.float32)
    halo_rows = 8 * (fields // 2) + (fields // 2 + 7) // 8 * 8
    ah, al = split_table(
        np.concatenate([pad_table(second[k], 88, 96) for k in range(3)], axis=0)
    )
    diag = np.zeros((88, LANES), np.float32)
    diag[:81] = penalty_weight * counts[:, None]

    field_shape = jax.ShapeDtypeStruct(velocity.shape, jnp.float32)
    halo_shape = jax.ShapeDtypeStruct((3, halo_rows, LANES), jnp.float32)
    native = velocity.transpose(0, 2, 1, 3).reshape(3, 81 * fields, LANES)
    native_shape = jax.ShapeDtypeStruct(native.shape, jnp.float32)
    native_spec = pl.BlockSpec((1, 81 * fields, LANES), lambda f: (f, 0, 0))
    field_spec = pl.BlockSpec((1, fields, 81, LANES), lambda f: (f, 0, 0, 0))
    halo_spec = pl.BlockSpec((1, halo_rows, LANES), lambda f: (f, 0, 0))
    smem = pl.BlockSpec(memory_space=pltpu.SMEM)

    def whole(shape):
        return pl.BlockSpec(shape, lambda f: (0,) * len(shape))

    params = pltpu.CompilerParams(vmem_limit_bytes=60 << 20)
    metric_spec, table_spec = whole((4, LANES)), whole((8, LANES))
    operator_specs = [
        smem,
        metric_spec,
        table_spec,
        whole((264, 96)),
        whole((264, 96)),
        whole((88, LANES)),
    ]
    ah_table, al_table, diag_table = (jnp.asarray(t) for t in (ah, al, diag))

    plane_z = basis @ z_derivative
    if packed:
        bh, bl = split_table(np.concatenate([basis, plane_z], axis=0))
        dh, dl = split_table(
            np.concatenate(
                [pad_table(along_r.T, 128, 128), pad_table(along_s.T, 128, 128)], axis=1
            )
        )
        ih, il = split_table(inverse)
        constants = np.zeros((1296, 256), ml_dtypes.bfloat16)
        constants[0:256] = np.concatenate([bh, bh], axis=1)
        constants[256:512] = np.concatenate([dh, dh], axis=0)
        constants[512:640] = np.concatenate([ih, ih], axis=1)
        constants[640:768] = dl
        constants[768:1024, 0:128] = bl
        constants[768:896, 128:256] = il
        constants[1024:1288, 0:96] = ah
        constants[1024:1288, 128:224] = al
        vmem = pl.BlockSpec(memory_space=pltpu.VMEM)
        hbm = pl.BlockSpec(memory_space=pltpu.HBM)
        halo_buffer = pltpu.VMEM((3, halo_rows, LANES), jnp.float32)
        trade_buffer = pltpu.VMEM((2, 8, 264, LANES), jnp.float32)
        state, advection, low, top, table = pl.pallas_call(
            functools.partial(fused_kernel, lax.axis_size("mesh")),
            in_specs=[smem] * 2 + [hbm] * 7,
            out_specs=[vmem] * 5,
            out_shape=[
                field_shape,
                field_shape,
                halo_shape,
                halo_shape,
                jax.ShapeDtypeStruct((8, LANES), jnp.int32),
            ],
            scratch_shapes=[
                pltpu.VMEM((4, LANES), jnp.float32),
                pltpu.VMEM((4, LANES), jnp.int32),
                pltpu.VMEM((2, LANES), jnp.int32),
                pltpu.VMEM(send_list.shape, jnp.int32),
                pltpu.VMEM(diag.shape, jnp.float32),
                pltpu.VMEM(constants.shape, jnp.bfloat16),
                pltpu.VMEM(native.shape, jnp.float32),
            ]
            + [trade_buffer] * 4
            + [pltpu.VMEM((1024, LANES), jnp.float32)] * 6
            + [pltpu.VMEM(velocity.shape, jnp.float32)]
            + [halo_buffer] * 6
            + [pltpu.SemaphoreType.DMA((2, 3, 8))] * 4
            + [pltpu.SemaphoreType.DMA((4, 2))] * 2
            + [pltpu.SemaphoreType.DMA((9,))],
            compiler_params=pltpu.CompilerParams(
                vmem_limit_bytes=60 << 20, collective_id=0, has_side_effects=True
            ),
        )(
            shifts,
            metrics,
            metrics,
            connect.T,
            recv_slot.T,
            send_list,
            jnp.asarray(diag),
            jnp.asarray(constants),
            native,
        )
    else:
        own = jnp.where(
            connect < 0, -1, jnp.clip(connect - mesh_index * elements, 0, elements - 1)
        )
        table = jnp.concatenate(
            [own.T, recv_slot.T, jnp.concatenate([send_list, send_list], axis=1)], axis=0
        )
        tables = [
            jnp.asarray(t, jnp.float32) for t in (along_r, along_s, basis, inverse, plane_z)
        ]
        advection = plain_advection(velocity, metrics, tables, mode_count)
        down, up = pl.pallas_call(
            functools.partial(halo_kernel, fields),
            grid=(3,),
            in_specs=[table_spec, native_spec],
            out_specs=[halo_spec, halo_spec],
            out_shape=[halo_shape, halo_shape],
            compiler_params=params,
        )(table, native)
        part = pl.pallas_call(
            functools.partial(first_kernel, fields),
            grid=(3,),
            in_specs=operator_specs + [native_spec, halo_spec, halo_spec],
            out_specs=field_spec,
            out_shape=field_shape,
            compiler_params=params,
        )(shifts, metrics, table, ah_table, al_table, diag_table, native, shifted(up, "mesh", 1), shifted(down, "mesh", -1))
        state, down, up = pl.pallas_call(
            functools.partial(state_kernel, fields),
            grid=(3,),
            in_specs=[smem, metric_spec, table_spec, field_spec, field_spec],
            out_specs=[field_spec, halo_spec, halo_spec],
            out_shape=[field_shape, halo_shape, halo_shape],
            compiler_params=params,
        )(shifts, metrics, table, advection, part)
        low = shifted(up, "mesh", 1)
        top = shifted(down, "mesh", -1)

    results = pl.pallas_call(
        functools.partial(last_kernel, fields),
        grid=(3,),
        in_specs=operator_specs + [field_spec, halo_spec, halo_spec, native_spec, field_spec],
        out_specs=[native_spec, native_spec],
        out_shape=[native_shape, native_shape],
        compiler_params=params,
    )(shifts, metrics, table, ah_table, al_table, diag_table, state, low, top, native, advection)
    return tuple(
        out.reshape(3, 81, fields, LANES).transpose(0, 2, 1, 3) for out in results
    )


def solution(mesh):
    return jax.shard_map(
        body,
        mesh=mesh,
        in_specs=(
            P(None, "modes", None, "mesh"),
            P(None, "mesh"),
            P("mesh", None),
            P("mesh", None),
            P("mesh", None),
        ),
        out_specs=(P(None, "modes", None, "mesh"), P(None, "modes", None, "mesh")),
        check_vma=False,
    )
```
